32 devices in a mesh: dp: 4 (over z), blk: 2 (over y), head: 4 (over x, core).
Axes of the slice: x: 2, y: 2, z: 4, core: 2. Of those that a mesh axis runs over, the one named last changes fastest.
Arguments:
- tokens: bfloat16 [4, 2048, 768], P('dp', ('blk', 'head')), may hold values from -6 to 6
- cond: bfloat16 [4, 128], P('dp'), may hold values from -6 to 6
- lengths: int32 [4], P('dp'), may hold values from 1024 to 2048, as said below
- ada_weight: bfloat16 [128, 4608], P(None, ('dp', 'blk', 'head')), may hold values from -0.5 to 0.5
- ada_bias: bfloat16 [4608], P(('dp', 'blk', 'head')), may hold values from -4 to 4
- norm1_gain: bfloat16 [768], P(('dp', 'blk', 'head')), may hold values from 0.5 to 1.5
- qkv_weight: bfloat16 [768, 2304], P(None, ('dp', 'blk', 'head')), may hold values from -0.15136719 to 0.15136719
- out_weight: bfloat16 [768, 768], P(None, ('dp', 'blk', 'head')), may hold values from -3.078125 to 3.078125
- norm2_gain: bfloat16 [768], P(('dp', 'blk', 'head')), may hold values from 0.5 to 1.5
- up_weight: bfloat16 [768, 3072], P(None, ('dp', 'blk', 'head')), may hold values from -0.21875 to 0.21875
- up_bias: bfloat16 [3072], P(('dp', 'blk', 'head')), may hold values from -4 to 4
- down_weight: bfloat16 [3072, 768], P(None, ('dp', 'blk', 'head')), may hold values from -0.109375 to 0.109375
- down_bias: bfloat16 [768], P(('dp', 'blk', 'head')), may hold values from -4 to 4
- out_grad: bfloat16 [4, 2048, 768], P('dp', ('blk', 'head')), may hold values from -6 to 6
Outputs:
- mixed: bfloat16 [4, 2048, 768], P('dp', ('blk', 'head'))
- tokens_grad: float32 [4, 2048, 768], P('dp', ('blk', 'head'))
- cond_grad: float32 [4, 128], P('dp')
- ada_weight_grad: float32 [128, 4608], P(None, ('dp', 'blk', 'head'))
- ada_bias_grad: float32 [4608], P(('dp', 'blk', 'head'))
- norm1_gain_grad: float32 [768], P(('dp', 'blk', 'head'))
- qkv_weight_grad: float32 [768, 2304], P(None, ('dp', 'blk', 'head'))
- out_weight_grad: float32 [768, 768], P(None, ('dp', 'blk', 'head'))
- norm2_gain_grad: float32 [768], P(('dp', 'blk', 'head'))
- up_weight_grad: float32 [768, 3072], P(None, ('dp', 'blk', 'head'))
- up_bias_grad: float32 [3072], P(('dp', 'blk', 'head'))
- down_weight_grad: float32 [3072, 768], P(None, ('dp', 'blk', 'head'))
- down_bias_grad: float32 [768], P(('dp', 'blk', 'head'))
The draws below stay inside these ranges and needn't reach their ends.
Inputs may be any that keep to these rules, and one draw needn't show every extreme that they name: Row r holds one sequence in its slots 0 to lengths[r] - 1, the rest is padding; some row is full and some row is half full.
All inputs are finite; a program needn't handle non-finite values.
Results may differ from the reference program's by a relative error of at most 0.034.
Values may be sent and summed in bfloat16 or wider, within the bound.
A program may use at most 128 MiB of HBM per device.

```python
import math
from functools import partial
import jax
import jax.numpy as jnp
from jax import lax

D = 768
HEADS = 12
HEAD_DIM = 64
FF = 3072
COND = 128
ROWS = 4
SLOTS = 2048


def draw_lengths(key, part):
    half_slots = SLOTS // 2
    first_key, second_key, third_key = jax.random.split(key, 3)
    drawn_lengths = jax.random.randint(first_key, (ROWS,), half_slots, SLOTS + 1, dtype=jnp.int32)
    full_row = jax.random.randint(second_key, (), 0, ROWS, dtype=jnp.int32)
    short_row = (full_row + 1 + jax.random.randint(third_key, (), 0, ROWS - 1, dtype=jnp.int32)) % ROWS
    row_ids = jnp.arange(ROWS, dtype=jnp.int32)
    drawn_lengths = jnp.where(row_ids == full_row, SLOTS, drawn_lengths)
    return jnp.where(row_ids == short_row, half_slots, drawn_lengths).astype(jnp.int32)


def steps_of(stream_key, dims, shards, smallest, high):
    gain = 1.0
    for axis_at, parts in shards:
        heights = jax.random.uniform(jax.random.fold_in(jax.random.fold_in(stream_key, 6), axis_at), (parts,), jnp.float32, smallest / len(shards), high / len(shards))
        gain = gain * jnp.repeat(jnp.exp(heights), dims[axis_at] // parts).reshape((-1,) + (1,) * (len(dims) - 1 - axis_at))
    return gain


def centred(key, dims, scale, most, cuts=(), kind=jnp.bfloat16):
    values = jax.random.normal(key, dims, jnp.float32) * scale
    if len(cuts) > 0:
        values = steps_of(key, dims, cuts, -0.22, 0.18) * values
    return jnp.clip(values, min=-most, max=most).astype(kind)


def setup_inputs(seed: int = 0) -> dict:
    streams_of = jax.random.split(jax.random.key(seed), 15)
    return {
        "tokens": centred(streams_of[0], (ROWS, SLOTS, D), 1.0, 6.0, ((0, 4), (1, 8))),
        "cond": centred(streams_of[1], (ROWS, COND), 1.0, 6.0, ((0, 4),)),
        "lengths": draw_lengths(jax.random.fold_in(streams_of[14], 71), 0),
        "ada_weight": centred(streams_of[3], (COND, 6 * D), COND ** -0.5, 0.5, ((1, 32),)),
        "ada_bias": centred(streams_of[4], (6 * D,), 0.3, 4.0, ((0, 32),)),
        "norm1_gain": jnp.clip(1.0 + 0.1 * jax.random.normal(streams_of[5], (D,), jnp.float32), 0.5, 1.5).astype(jnp.bfloat16),
        "qkv_weight": centred(streams_of[6], (D, 3 * D), (0.7 * D ** -0.5), 0.15136719, ((1, 32),)),
        "out_weight": centred(streams_of[7], (D, D), ((SLOTS // 10) ** 0.5 * D ** -0.5), 3.078125, ((1, 32),)),
        "norm2_gain": jnp.clip(1.0 + 0.1 * jax.random.normal(streams_of[8], (D,), jnp.float32), 0.5, 1.5).astype(jnp.bfloat16),
        "up_weight": centred(streams_of[9], (D, FF), D ** -0.5, 0.21875, ((1, 32),)),
        "up_bias": centred(streams_of[10], (FF,), 0.3, 4.0, ((0, 32),)),
        "down_weight": centred(streams_of[11], (FF, D), FF ** -0.5, 0.109375, ((1, 32),)),
        "down_bias": centred(streams_of[12], (D,), 0.3, 4.0, ((0, 32),)),
        "out_grad": centred(streams_of[13], (ROWS, SLOTS, D), 1.0, 6.0, ((0, 4), (1, 8))),
    }


EPSILON = 1e-05
NEG_LARGE = -1e+30
HIGHEST = lax.Precision.HIGHEST

@jax.custom_vjp
def low(v):
    return lax.optimization_barrier(v.astype(jnp.bfloat16)).astype(jnp.float32)

@jax.custom_vjp
def low_back(v):
    return v

def low_keep(v):
    return (low(v), None)

def low_pass(kept, grad):
    return (grad,)

def back_keep(v):
    return (v, None)

def back_low(kept, grad):
    return (low(grad),)
low.defvjp(low_keep, low_pass)
low_back.defvjp(back_keep, back_low)

def layer_norm(values, norm_gain):
    center = values - lax.optimization_barrier(jnp.mean(values, axis=-1, keepdims=True))
    spread = lax.optimization_barrier(jnp.mean(center * center, axis=-1, keepdims=True))
    return center * lax.rsqrt(spread + EPSILON) * norm_gain

def rotary_tables(positions):
    half_dim = HEAD_DIM // 2
    frequency = jnp.exp(jnp.arange(half_dim, dtype=jnp.float32) * (-2.0 * math.log(10000.0) / HEAD_DIM))
    angles = positions.astype(jnp.float32)[:, None] * frequency[None, :]
    return (jnp.cos(angles), jnp.sin(angles))

def rotate(values, cosine, sine):
    half_dim = HEAD_DIM // 2
    first_half = values[..., :half_dim]
    second_half = values[..., half_dim:]
    cos_wide = cosine[:, None, :]
    sin_wide = sine[:, None, :]
    return jnp.concatenate([first_half * cos_wide - second_half * sin_wide, second_half * cos_wide + first_half * sin_wide], axis=-1)

def attend_row(operands):
    queries, key_rows, value_rows, length = operands
    key_live = jnp.arange(SLOTS, dtype=jnp.int32) < length
    score_scale = HEAD_DIM ** (-0.5)

    def one_block(query_block):
        scores = jnp.einsum('qhd,khd->hqk', query_block, key_rows, precision=HIGHEST) * score_scale
        scores = low_back(scores)
        scores = jnp.where(key_live[None, None, :], scores, NEG_LARGE)
        row_peak = lax.optimization_barrier(jnp.max(scores, axis=-1, keepdims=True))
        weights = jnp.where(key_live[None, None, :], jnp.exp(scores - row_peak), 0.0)
        weights_low = low(weights / lax.optimization_barrier(jnp.sum(weights, axis=-1, keepdims=True)))
        return jnp.einsum('hqk,khd->qhd', weights_low, value_rows, precision=HIGHEST)
    block_rows = min(SLOTS, 512)
    blocks = queries.reshape(SLOTS // block_rows, block_rows, HEADS, HEAD_DIM)
    return lax.map(jax.checkpoint(one_block), blocks).reshape(SLOTS, HEADS, HEAD_DIM)

def forward(lengths, tokens, cond, ada_weight, ada_bias, norm1_gain, qkv_weight, out_weight, norm2_gain, up_weight, up_bias, down_weight, down_bias):
    modulation = jnp.dot(cond, ada_weight, precision=HIGHEST) + ada_bias
    pieces = [modulation[:, None, part_index * D:(part_index + 1) * D] for part_index in range(6)]
    shift_one, scale_one, gate_one, shift_two, scale_two, gate_two = pieces
    hidden_one = low(layer_norm(tokens, norm1_gain) * (1.0 + scale_one) + shift_one)
    projected = low_back(jnp.einsum('rsd,de->rse', hidden_one, qkv_weight, precision=HIGHEST))
    projected = projected.reshape(ROWS, SLOTS, 3, HEADS, HEAD_DIM)
    cosine, sine = rotary_tables(jnp.arange(SLOTS, dtype=jnp.int32))
    queries = low(low_back(rotate(projected[:, :, 0], cosine, sine)))
    key_rows = low(low_back(rotate(projected[:, :, 1], cosine, sine)))
    value_rows = low(low_back(projected[:, :, 2]))
    attended = lax.map(attend_row, (queries, key_rows, value_rows, lengths))
    attended = low(low_back(attended.reshape(ROWS, SLOTS, D)))
    branch_one = low_back(jnp.einsum('rsd,de->rse', attended, out_weight, precision=HIGHEST))
    middle = tokens + gate_one * branch_one
    hidden_two = low(layer_norm(middle, norm2_gain) * (1.0 + scale_two) + shift_two)
    inner = low_back(jnp.einsum('rsd,df->rsf', hidden_two, up_weight, precision=HIGHEST) + up_bias)
    activated = low(jax.nn.gelu(inner, approximate=True))
    branch_two = low_back(jnp.einsum('rsf,fd->rsd', activated, down_weight, precision=HIGHEST) + down_bias)
    return middle + gate_two * branch_two

def reference(tokens, cond, lengths, ada_weight, ada_bias, norm1_gain, qkv_weight, out_weight, norm2_gain, up_weight, up_bias, down_weight, down_bias, out_grad):
    inputs = (tokens, cond, ada_weight, ada_bias, norm1_gain, qkv_weight, out_weight, norm2_gain, up_weight, up_bias, down_weight, down_bias)
    widened = [array_in.astype(jnp.float32) for array_in in inputs]
    result, pullback = jax.vjp(partial(forward, lengths), *widened)
    slot_live = (jnp.arange(SLOTS, dtype=jnp.int32)[None, :] < lengths[:, None]).astype(jnp.float32)
    cotangent = out_grad.astype(jnp.float32) * slot_live[..., None]
    grads = pullback(cotangent)
    return (result.astype(jnp.bfloat16), grads[0], grads[1], grads[2], grads[3], grads[4], grads[5], grads[6], grads[7], grads[8], grads[9], grads[10], grads[11])
```

```python
from functools import partial
import math

import jax
import jax.numpy as jnp
from jax import lax
from jax.experimental import pallas as pl
from jax.experimental.pallas import tpu as pltpu
from jax.sharding import PartitionSpec as P

AXES=("dp","blk","head")
MESHID = pl.DeviceIdType.MESH

def log2(n):
    assert n & (n-1) == 0
    return n.bit_length()-1

class Topo:
    def __init__(self, mesh):
        self.nd, self.nb, self.nh = (mesh.shape[a] for a in AXES)
        self.n = self.nd*self.nb*self.nh
        lh, lb, ld = log2(self.nh), log2(self.nb), log2(self.nd)
        head=list(range(lh)); blk=list(range(lh,lh+lb)); dp=list(range(lh+lb,lh+lb+ld))
        self.orders = (dp+blk+head[1:]+head[:1], dp+head[1:]+blk+head[:1])
        self.phases = lh+lb+ld
    def here(self):
        return (lax.axis_index("dp")*self.nb+lax.axis_index("blk"))*self.nh+lax.axis_index("head")
    def coords(self, i):
        return (i//(self.nb*self.nh), (i//self.nh)%self.nb, i%self.nh)
    def deltas(self, me, color=None):
        color = me % 2 if color is None else color
        d=[]
        for p in range(self.phases):
            a,b=self.orders[0][p],self.orders[1][p]
            da=(1-2*((me//2**a)%2))*2**a
            if a==b: d.append(da)
            else:
                db=(1-2*((me//2**b)%2))*2**b
                d.append(da+color*(db-da))
        return d

def gather_kernel(topo, count, *refs):
    ins=refs[:count]; outs=refs[count:2*count]; send,recv,local=refs[2*count:]
    me=topo.here(); delta=topo.deltas(me); ph=topo.phases; other=topo.deltas(me,1-me%2)
    def block(a):
        b=me
        use=other if a>>(ph-1)&1 else delta
        for k in range(ph):
            if a>>k&1: b=b+use[k]
        return b
    partner=[topo.coords(me+d) for d in delta]
    barrier=pltpu.get_barrier_semaphore()
    for pr in partner: pl.semaphore_signal(barrier,1,device_id=pr,device_id_type=MESHID)
    pl.semaphore_wait(barrier,ph)
    def copy(k,a,p,src):
        blkid=block(a)
        arr=a+2**p
        return pltpu.make_async_remote_copy(src_ref=src if a==0 else outs[k].at[blkid], dst_ref=outs[k].at[blkid],
            send_sem=send.at[k,arr], recv_sem=recv.at[k,arr], device_id=partner[p], device_id_type=MESHID)
    sends=[]
    for k in range(count):
        for p in range(ph):
            c=copy(k,0,p,ins[k]); c.start(); sends.append(c)
    locs=[]
    for k in range(count):
        c=pltpu.make_async_copy(ins[k],outs[k].at[me],local.at[k]); c.start(); locs.append(c)
    for a in range(1,2**ph):
        top=a.bit_length()-1
        for k in range(count):
            blkid=block(a)
            w=pltpu.make_async_remote_copy(src_ref=outs[k].at[blkid],dst_ref=outs[k].at[blkid],send_sem=send.at[k,a],recv_sem=recv.at[k,a],device_id=partner[top],device_id_type=MESHID)
            w.wait_recv()
            for p in range(top+1,ph):
                c=copy(k,a,p,None); c.start(); sends.append(c)
    for c in sends: c.wait_send()
    for c in locs: c.wait()

def gather(topo, arrays, cid):
    n=topo.n; k=len(arrays)
    return pl.pallas_call(
        partial(gather_kernel,topo,k),
        out_shape=[jax.ShapeDtypeStruct((n,)+a.shape,a.dtype) for a in arrays],
        in_specs=[pl.BlockSpec(memory_space=pltpu.VMEM)]*k,
        out_specs=[pl.BlockSpec(memory_space=pl.ANY)]*k,
        scratch_shapes=[pltpu.SemaphoreType.DMA((k,n)),pltpu.SemaphoreType.DMA((k,n)),pltpu.SemaphoreType.DMA((k,))],
        compiler_params=pltpu.CompilerParams(collective_id=cid,has_side_effects=True),
        name="gather%d"%cid)(*arrays)

def reduce_kernel(topo, count, *refs):
    ins=refs[:count]; outs=refs[count:2*count]; arrs=refs[2*count:3*count]; send,recv=refs[3*count:]
    me=topo.here(); delta=topo.deltas(me); ph=topo.phases; other=topo.deltas(me,1-me%2)
    def block(a):
        b=me
        use=other if a>>(ph-1)&1 else delta
        for k in range(ph):
            if a>>k&1: b=b+use[k]
        return b
    partner=[topo.coords(me+d) for d in delta]
    barrier=pltpu.get_barrier_semaphore()
    for pr in partner: pl.semaphore_signal(barrier,1,device_id=pr,device_id_type=MESHID)
    pl.semaphore_wait(barrier,ph)
    def copy(k,a,src):
        t=a.bit_length()-1
        return pltpu.make_async_remote_copy(src_ref=src,dst_ref=arrs[k].at[a],send_sem=send.at[k,a],recv_sem=recv.at[k,a],
            device_id=partner[t],device_id_type=MESHID)
    sends=[]
    half=2**(ph-1)
    for a in range(2**ph-1,half-1,-1):
        for k in range(count):
            c=copy(k,a,ins[k].at[block(a)]); c.start(); sends.append(c)
    for a in range(half-1,-1,-1):
        t=a.bit_length()-1
        for k in range(count):
            total=ins[k][block(a)].astype(jnp.float32)
            for p in range(ph-1,t,-1):
                idx=2**p+a
                copy(k,idx,arrs[k].at[idx]).wait_recv()
                total=total+arrs[k][idx].astype(jnp.float32)
            if a==0:
                outs[k][...]=total
            else:
                slot=arrs[k].at[half+a]
                slot[...]=total.astype(slot.dtype)
                c=copy(k,a,slot); c.start(); sends.append(c)
    for c in sends: c.wait_send()

def reduce_scatter(topo, arrays, cid):
    n=topo.n; k=len(arrays)
    return pl.pallas_call(
        partial(reduce_kernel,topo,k),
        out_shape=[jax.ShapeDtypeStruct(a.shape[1:],jnp.float32) for a in arrays],
        in_specs=[pl.BlockSpec(memory_space=pltpu.VMEM)]*k,
        out_specs=[pl.BlockSpec(memory_space=pltpu.VMEM)]*k,
        scratch_shapes=[pltpu.VMEM(a.shape,a.dtype) for a in arrays]+[pltpu.SemaphoreType.DMA((k,n)),pltpu.SemaphoreType.DMA((k,n))],
        compiler_params=pltpu.CompilerParams(collective_id=cid,has_side_effects=True,vmem_limit_bytes=60*2**20),
        name="reduce%d"%cid)(*arrays)


HEADS = 12
HEAD_DIM = 64


EPSILON = 1e-05
NEG_LARGE = -1e30
HIGHEST = lax.Precision.HIGHEST


def rotary_tables(positions):
    half_dim = HEAD_DIM // 2
    frequency = jnp.exp(
        jnp.arange(half_dim, dtype=jnp.float32) * (-2.0 * math.log(10000.0) / HEAD_DIM)
    )
    angles = positions.astype(jnp.float32)[:, None] * frequency[None, :]
    return (jnp.cos(angles), jnp.sin(angles))


def rotate(values, cosine, sine):
    half_dim = HEAD_DIM // 2
    first_half = values[..., :half_dim]
    second_half = values[..., half_dim:]
    cos_wide = cosine[:, None, :]
    sin_wide = sine[:, None, :]
    return jnp.concatenate(
        [
            first_half * cos_wide - second_half * sin_wide,
            second_half * cos_wide + first_half * sin_wide,
        ],
        axis=-1,
    )


def rotate_back(grads, cosine, sine):
    half_dim = HEAD_DIM // 2
    first_half = grads[..., :half_dim]
    second_half = grads[..., half_dim:]
    cos_wide = cosine[:, None, :]
    sin_wide = sine[:, None, :]
    return jnp.concatenate(
        [
            first_half * cos_wide + second_half * sin_wide,
            second_half * cos_wide - first_half * sin_wide,
        ],
        axis=-1,
    )


def normalize(values):
    center = values - jnp.mean(values, axis=-1, keepdims=True)
    inverse = lax.rsqrt(jnp.mean(center * center, axis=-1, keepdims=True) + EPSILON)
    return (center * inverse, inverse)


def normalize_back(grad_unit, unit_values, inverse):
    mean_grad = jnp.mean(grad_unit, axis=-1, keepdims=True)
    mean_cross = jnp.mean(grad_unit * unit_values, axis=-1, keepdims=True)
    return (grad_unit - mean_grad - unit_values * mean_cross) * inverse


def block_size(count_rows):
    return math.gcd(count_rows, 1024)


def key_window(piece_array, offset, step_rows, heads_local):
    window = lax.dynamic_slice_in_dim(piece_array, offset, step_rows, 1)
    return window.reshape(window.shape[0], step_rows, heads_local, HEAD_DIM)


def score_grads(
    query_block, grad_block, key_block, value_block, log_block, delta_block, key_live, score_scale
):
    scores = (
        jnp.einsum("rqhd,rkhd->rhqk", query_block, key_block, preferred_element_type=jnp.float32)
        * score_scale
    )
    probs = jnp.where(key_live, jnp.exp(scores - log_block[..., None]), 0.0)
    grad_probs = jnp.einsum(
        "rqhd,rkhd->rhqk", grad_block, value_block, preferred_element_type=jnp.float32
    )
    grad_scores = (probs * (grad_probs - delta_block[..., None])).astype(jnp.bfloat16)
    return (probs.astype(jnp.bfloat16), grad_scores)


def attend_fold(queries, lengths, score_scale, running, piece_rows):
    heads_local = queries.shape[2]
    key_piece, value_piece = piece_rows
    piece_len = key_piece.shape[1]
    step_rows = block_size(piece_len)

    def attend_one_step(step_index, loop_state):
        row_peak, row_total, summed = loop_state
        offset = step_index * step_rows
        key_block = key_window(key_piece, offset, step_rows, heads_local)
        value_block = key_window(value_piece, offset, step_rows, heads_local)
        positions = offset + jnp.arange(step_rows, dtype=jnp.int32)
        key_live = (positions[None, :] < lengths[:, None])[:, None, None, :]
        scores = (
            jnp.einsum("rqhd,rkhd->rhqk", queries, key_block, preferred_element_type=jnp.float32)
            * score_scale
        )
        scores = jnp.where(key_live, scores, NEG_LARGE)
        new_peak = jnp.maximum(row_peak, jnp.max(scores, axis=-1))
        weights = jnp.where(key_live, jnp.exp(scores - new_peak[..., None]), 0.0)
        fade_factor = jnp.exp(row_peak - new_peak)
        row_total = row_total * fade_factor + jnp.sum(weights, axis=-1)
        update = jnp.einsum(
            "rhqk,rkhd->rqhd",
            weights.astype(jnp.bfloat16),
            value_block,
            preferred_element_type=jnp.float32,
        )
        summed = summed * jnp.transpose(fade_factor, (0, 2, 1))[..., None] + update
        return (new_peak, row_total, summed)

    return lax.fori_loop(0, piece_len // step_rows, attend_one_step, running)


def query_fold(
    queries, grad_heads, log_total, row_delta, lengths, score_scale, running, piece_rows
):
    heads_local = queries.shape[2]
    key_piece, value_piece = piece_rows
    piece_len = key_piece.shape[1]
    step_rows = block_size(piece_len)

    def query_one_step(step_index, grad_query):
        offset = step_index * step_rows
        key_block = key_window(key_piece, offset, step_rows, heads_local)
        value_block = key_window(value_piece, offset, step_rows, heads_local)
        positions = offset + jnp.arange(step_rows, dtype=jnp.int32)
        key_live = (positions[None, :] < lengths[:, None])[:, None, None, :]
        probs_low, grad_scores = score_grads(
            queries, grad_heads, key_block, value_block, log_total, row_delta, key_live, score_scale
        )
        return (
            grad_query
            + jnp.einsum(
                "rhqk,rkhd->rqhd", grad_scores, key_block, preferred_element_type=jnp.float32
            )
            * score_scale
        )

    return lax.fori_loop(0, piece_len // step_rows, query_one_step, running)


def key_fold(
    key_heads, value_heads, key_live, stat_logs, stat_deltas, score_scale, running, piece_rows
):
    heads_local = key_heads.shape[2]
    query_piece, grad_piece = piece_rows
    piece_len = query_piece.shape[1]
    step_rows = block_size(piece_len)

    def key_one_step(step_index, loop_state):
        grad_key, grad_value = loop_state
        offset = step_index * step_rows
        query_block = key_window(query_piece, offset, step_rows, heads_local)
        grad_block = key_window(grad_piece, offset, step_rows, heads_local)
        log_block = jnp.transpose(
            lax.dynamic_slice_in_dim(stat_logs, offset, step_rows, 1), (0, 2, 1)
        )
        delta_block = jnp.transpose(
            lax.dynamic_slice_in_dim(stat_deltas, offset, step_rows, 1), (0, 2, 1)
        )
        probs_low, grad_scores = score_grads(
            query_block,
            grad_block,
            key_heads,
            value_heads,
            log_block,
            delta_block,
            key_live,
            score_scale,
        )
        grad_key = (
            grad_key
            + jnp.einsum(
                "rhqk,rqhd->rkhd", grad_scores, query_block, preferred_element_type=jnp.float32
            )
            * score_scale
        )
        grad_value = grad_value + jnp.einsum(
            "rhqk,rqhd->rkhd", probs_low, grad_block, preferred_element_type=jnp.float32
        )
        return (grad_key, grad_value)

    return lax.fori_loop(0, piece_len // step_rows, key_one_step, running)


def body(
    topo,
    tokens,
    cond,
    lengths,
    ada_weight,
    ada_bias,
    norm1_gain,
    qkv_weight,
    out_weight,
    norm2_gain,
    up_weight,
    up_bias,
    down_weight,
    down_bias,
    out_grad,
):
    devices = topo.n
    rows_all = topo.nd
    float_type = jnp.float32
    cond_all = lax.all_gather(cond, "dp", axis=0, tiled=True)
    mod_columns = ada_weight.shape[1]
    mod_own = jnp.dot(cond_all, ada_weight, preferred_element_type=float_type) + ada_bias.astype(
        float_type
    )
    vectors = [norm1_gain, norm2_gain, up_bias, down_bias]
    small = jnp.concatenate(
        [mod_own.reshape(-1)] + [v.astype(float_type) for v in vectors]
    )
    small_used = small.shape[0]
    small = jnp.pad(small, (0, -small_used % 1024)).reshape(-1, 128)
    small_all, qkv_t, out_t, up_t, down_t, ada_t = gather(
        topo, [small, qkv_weight.T, out_weight.T, up_weight.T, down_weight.T, ada_weight.T], 0
    )
    qkv_t = qkv_t.reshape(-1, qkv_t.shape[-1])
    out_t = out_t.reshape(-1, out_t.shape[-1])
    up_t = up_t.reshape(-1, up_t.shape[-1])
    down_t = down_t.reshape(-1, down_t.shape[-1])
    ada_t = ada_t.reshape(-1, ada_t.shape[-1])
    small_all = small_all.reshape(devices, -1)
    mod_all = small_all[:, : rows_all * mod_columns].reshape(devices, rows_all, mod_columns)
    modulation = lax.dynamic_index_in_dim(
        mod_all, lax.axis_index("dp"), 1, keepdims=False
    ).reshape(1, -1)
    cut = rows_all * mod_columns
    full_vectors = []
    for v in vectors:
        full_vectors.append(small_all[:, cut : cut + v.shape[0]].reshape(-1))
        cut += v.shape[0]
    gain_one, gain_two, up_bias_full, down_bias_full = full_vectors
    row_count, tok_count, width = tokens.shape
    head_groups = lax.axis_size("head")
    heads_local = HEADS // head_groups
    local_width = heads_local * HEAD_DIM
    group_rows = tok_count * head_groups
    score_scale = HEAD_DIM ** (-0.5)
    pieces = [
        modulation[:, None, part_index * width : (part_index + 1) * width]
        for part_index in range(6)
    ]
    shift_one, scale_one, gate_one, shift_two, scale_two, gate_two = pieces
    seq_index = lax.axis_index("blk") * head_groups + lax.axis_index("head")
    positions = seq_index * tok_count + jnp.arange(tok_count, dtype=jnp.int32)
    slot_live = (positions[None, :] < lengths[:, None]).astype(float_type)[..., None]
    cosine, sine = rotary_tables(positions)
    tokens_wide = tokens.astype(float_type)
    unit_one, inverse_one = normalize(tokens_wide)
    normed_one = unit_one * gain_one.astype(float_type)
    hidden_one = (normed_one * (1.0 + scale_one) + shift_one).astype(jnp.bfloat16)
    projected = jnp.einsum("rtd,ed->rte", hidden_one, qkv_t, preferred_element_type=float_type)
    projected = projected.reshape(row_count, tok_count, 3, HEADS, HEAD_DIM)
    turned = jnp.stack(
        [
            rotate(projected[:, :, 0], cosine, sine),
            rotate(projected[:, :, 1], cosine, sine),
            projected[:, :, 2],
        ],
        axis=2,
    ).astype(jnp.bfloat16)
    grouped = lax.all_to_all(
        turned.reshape(row_count, tok_count, 3, head_groups, local_width),
        "head",
        split_axis=3,
        concat_axis=1,
        tiled=True,
    )
    query_heads = grouped[:, :, 0, 0].reshape(row_count, group_rows, heads_local, HEAD_DIM)
    key_heads = grouped[:, :, 1, 0]
    value_heads = grouped[:, :, 2, 0]
    start_state = (
        jnp.full((row_count, heads_local, group_rows), NEG_LARGE, float_type),
        jnp.zeros((row_count, heads_local, group_rows), float_type),
        jnp.zeros((row_count, group_rows, heads_local, HEAD_DIM), float_type),
    )
    row_peak, row_total, summed = attend_fold(
        query_heads,
        lengths,
        score_scale,
        start_state,
        (
            lax.all_gather(key_heads, "blk", axis=1, tiled=True),
            lax.all_gather(value_heads, "blk", axis=1, tiled=True),
        ),
    )
    attended_heads = summed / jnp.transpose(row_total, (0, 2, 1))[..., None]
    log_total = row_peak + jnp.log(row_total)
    attended_low = attended_heads.astype(jnp.bfloat16).reshape(
        row_count, group_rows, 1, local_width
    )
    attended_seq = lax.all_to_all(
        attended_low, "head", split_axis=1, concat_axis=2, tiled=True
    ).reshape(row_count, tok_count, width)
    branch_one = jnp.einsum(
        "rtd,ed->rte", attended_seq, out_t, preferred_element_type=float_type
    )
    middle = tokens_wide + gate_one * branch_one
    unit_two, inverse_two = normalize(middle)
    normed_two = unit_two * gain_two.astype(float_type)
    hidden_two = (normed_two * (1.0 + scale_two) + shift_two).astype(jnp.bfloat16)
    inner = jnp.einsum(
        "rtd,fd->rtf", hidden_two, up_t, preferred_element_type=float_type
    ) + up_bias_full.astype(float_type)
    activated, gelu_back = jax.vjp(partial(jax.nn.gelu, approximate=True), inner)
    activated_low = activated.astype(jnp.bfloat16)
    branch_two = jnp.einsum(
        "rtf,df->rtd", activated_low, down_t, preferred_element_type=float_type
    ) + down_bias_full.astype(float_type)
    result = middle + gate_two * branch_two
    grad_out = out_grad.astype(float_type) * slot_live
    grad_gate_two = jnp.sum(grad_out * branch_two, axis=1)
    grad_branch_two = (grad_out * gate_two).astype(jnp.bfloat16)
    grad_down = jnp.einsum(
        "rtd,rtf->df", grad_branch_two, activated_low, preferred_element_type=float_type
    )
    grad_down_bias = jnp.sum(grad_branch_two.astype(float_type), axis=(0, 1))
    grad_activated = jnp.einsum(
        "rtd,df->rtf", grad_branch_two, down_t, preferred_element_type=float_type
    )
    grad_inner = gelu_back(grad_activated)[0].astype(jnp.bfloat16)
    grad_up = jnp.einsum("rtf,rtd->fd", grad_inner, hidden_two, preferred_element_type=float_type)
    grad_up_bias = jnp.sum(grad_inner.astype(float_type), axis=(0, 1))
    grad_hidden_two = jnp.einsum(
        "rtf,fd->rtd", grad_inner, up_t, preferred_element_type=float_type
    )
    grad_shift_two = jnp.sum(grad_hidden_two, axis=1)
    grad_scale_two = jnp.sum(grad_hidden_two * normed_two, axis=1)
    grad_normed_two = grad_hidden_two * (1.0 + scale_two)
    grad_gain_two = jnp.sum(grad_normed_two * unit_two, axis=(0, 1))
    grad_middle = grad_out + normalize_back(
        grad_normed_two * gain_two.astype(float_type), unit_two, inverse_two
    )
    grad_gate_one = jnp.sum(grad_middle * branch_one, axis=1)
    grad_branch_one = (grad_middle * gate_one).astype(jnp.bfloat16)
    grad_out_proj = jnp.einsum(
        "rte,rtd->ed", grad_branch_one, attended_seq, preferred_element_type=float_type
    )
    grad_attended = jnp.einsum(
        "rte,ed->rtd", grad_branch_one, out_t, preferred_element_type=float_type
    ).astype(jnp.bfloat16)
    grad_heads = lax.all_to_all(
        grad_attended.reshape(row_count, tok_count, head_groups, local_width),
        "head",
        split_axis=2,
        concat_axis=1,
        tiled=True,
    )
    grad_heads = grad_heads.reshape(row_count, group_rows, heads_local, HEAD_DIM)
    row_delta = jnp.transpose(
        jnp.sum(grad_heads.astype(float_type) * attended_heads, axis=-1), (0, 2, 1)
    )
    zero_heads = jnp.zeros((row_count, group_rows, heads_local, HEAD_DIM), float_type)
    stat_logs, stat_deltas = (
        lax.all_gather(jnp.transpose(log_total, (0, 2, 1)), "blk", axis=1, tiled=True),
        lax.all_gather(jnp.transpose(row_delta, (0, 2, 1)), "blk", axis=1, tiled=True),
    )
    grad_query = query_fold(
        query_heads,
        grad_heads,
        log_total,
        row_delta,
        lengths,
        score_scale,
        zero_heads,
        (
            lax.all_gather(key_heads, "blk", axis=1, tiled=True),
            lax.all_gather(value_heads, "blk", axis=1, tiled=True),
        ),
    )
    key_positions = lax.axis_index("blk") * group_rows + jnp.arange(group_rows, dtype=jnp.int32)
    key_live = (key_positions[None, :] < lengths[:, None])[:, None, None, :]
    key_four = key_heads.reshape(row_count, group_rows, heads_local, HEAD_DIM)
    value_four = value_heads.reshape(row_count, group_rows, heads_local, HEAD_DIM)
    grad_key, grad_value = key_fold(
        key_four,
        value_four,
        key_live,
        stat_logs,
        stat_deltas,
        score_scale,
        (zero_heads, zero_heads),
        (
            lax.all_gather(
                query_heads.reshape(row_count, group_rows, local_width), "blk", axis=1, tiled=True
            ),
            lax.all_gather(
                grad_heads.reshape(row_count, group_rows, local_width), "blk", axis=1, tiled=True
            ),
        ),
    )
    grad_stack = jnp.stack(
        [
            grad_query.reshape(row_count, group_rows, local_width),
            grad_key.reshape(row_count, group_rows, local_width),
            grad_value.reshape(row_count, group_rows, local_width),
        ],
        axis=2,
    ).astype(jnp.bfloat16)
    grad_seq = lax.all_to_all(
        grad_stack.reshape(row_count, group_rows, 3, 1, local_width),
        "head",
        split_axis=1,
        concat_axis=3,
        tiled=True,
    )
    grad_seq = grad_seq.astype(float_type).reshape(row_count, tok_count, 3, HEADS, HEAD_DIM)
    grad_projected = jnp.stack(
        [
            rotate_back(grad_seq[:, :, 0], cosine, sine),
            rotate_back(grad_seq[:, :, 1], cosine, sine),
            grad_seq[:, :, 2],
        ],
        axis=2,
    )
    grad_projected = grad_projected.reshape(row_count, tok_count, 3 * width).astype(jnp.bfloat16)
    grad_qkv = jnp.einsum(
        "rte,rtd->ed", grad_projected, hidden_one, preferred_element_type=float_type
    )
    grad_hidden_one = jnp.einsum(
        "rte,ed->rtd", grad_projected, qkv_t, preferred_element_type=float_type
    )
    grad_shift_one = jnp.sum(grad_hidden_one, axis=1)
    grad_scale_one = jnp.sum(grad_hidden_one * normed_one, axis=1)
    grad_normed_one = grad_hidden_one * (1.0 + scale_one)
    grad_gain_one = jnp.sum(grad_normed_one * unit_one, axis=(0, 1))
    grad_tokens = grad_middle + normalize_back(
        grad_normed_one * gain_one.astype(float_type), unit_one, inverse_one
    )
    grad_modulation = jnp.concatenate(
        [
            grad_shift_one,
            grad_scale_one,
            grad_gate_one,
            grad_shift_two,
            grad_scale_two,
            grad_gate_two,
        ],
        axis=-1,
    )
    cond_part = jnp.dot(
        grad_modulation, ada_t.astype(float_type), precision=HIGHEST
    ).reshape(1, -1)
    plane = jnp.arange(devices, dtype=jnp.int32) // (topo.nb * topo.nh) == lax.axis_index("dp")
    row_here = jnp.arange(rows_all, dtype=jnp.int32) == lax.axis_index("dp")
    mod_blocks = jnp.where(
        row_here[None, :, None], grad_modulation.reshape(devices, 1, mod_columns), 0.0
    )
    small_grads = jnp.concatenate(
        [mod_blocks.reshape(devices, -1)]
        + [
            v.reshape(devices, -1)
            for v in (grad_gain_one, grad_gain_two, grad_up_bias, grad_down_bias)
        ]
        + [jnp.where(plane[:, None], cond_part, 0.0)],
        axis=1,
    )
    used = small_grads.shape[1]
    small_grads = jnp.pad(small_grads, ((0, 0), (0, -used % 1024))).reshape(devices, -1, 128)
    small_own, qkv_own, out_own, up_own, down_own = reduce_scatter(
        topo,
        [small_grads]
        + [
            g.astype(jnp.bfloat16).reshape(devices, -1, g.shape[-1])
            for g in (grad_qkv, grad_out_proj, grad_up, grad_down)
        ],
        1,
    )
    small_own = small_own.reshape(-1)
    mod_grads = small_own[: rows_all * mod_columns].reshape(rows_all, mod_columns)
    cut = rows_all * mod_columns
    vector_grads = []
    for v in vectors:
        vector_grads.append(small_own[cut : cut + v.shape[0]])
        cut += v.shape[0]
    grad_cond = small_own[cut : cut + cond.shape[1]].reshape(1, -1)
    grad_ada = jnp.dot(cond_all.astype(float_type).T, mod_grads, precision=HIGHEST)
    return (
        result.astype(jnp.bfloat16),
        grad_tokens,
        grad_cond,
        grad_ada,
        jnp.sum(mod_grads, axis=0),
        vector_grads[0],
        qkv_own.T,
        out_own.T,
        vector_grads[1],
        up_own.T,
        vector_grads[2],
        down_own.T,
        vector_grads[3],
    )


def solution(mesh):
    placed = (
        P("dp", ("blk", "head"), None),
        P("dp", None),
        P("dp"),
        P(None, ("dp", "blk", "head")),
        P(("dp", "blk", "head")),
        P(("dp", "blk", "head")),
        P(None, ("dp", "blk", "head")),
        P(None, ("dp", "blk", "head")),
        P(("dp", "blk", "head")),
        P(None, ("dp", "blk", "head")),
        P(("dp", "blk", "head")),
        P(None, ("dp", "blk", "head")),
        P(("dp", "blk", "head")),
        P("dp", ("blk", "head"), None),
    )
    return jax.shard_map(
        partial(body, Topo(mesh)),
        mesh=mesh,
        in_specs=placed,
        out_specs=(
            P("dp", ("blk", "head"), None),
            P("dp", ("blk", "head"), None),
            P("dp", None),
            P(None, ("dp", "blk", "head")),
            P(("dp", "blk", "head")),
            P(("dp", "blk", "head")),
            P(None, ("dp", "blk", "head")),
            P(None, ("dp", "blk", "head")),
            P(("dp", "blk", "head")),
            P(None, ("dp", "blk", "head")),
            P(("dp", "blk", "head")),
            P(None, ("dp", "blk", "head")),
            P(("dp", "blk", "head")),
        ),
        check_vma=False,
    )
```

```python
from functools import partial
import math

import jax
import jax.numpy as jnp
from jax import lax
from jax.experimental import pallas as pl
from jax.experimental.pallas import tpu as pltpu
from jax.sharding import PartitionSpec as P

HEADS = 12
HEAD_DIM = 64
EPSILON = 1e-05
NEG_LARGE = -1e30
HIGHEST = lax.Precision.HIGHEST
F32 = jnp.float32
BF16 = jnp.bfloat16
AXES = ("dp", "blk", "head")
MESH_ID = pl.DeviceIdType.MESH
SCORE_SCALE = HEAD_DIM ** (-0.5)
EXP2_SCALE = SCORE_SCALE * math.log2(math.e)
VMEM_LIMIT = 60 * 2**20


def log2_of(count):
    assert count & (count - 1) == 0
    return count.bit_length() - 1


class Topo:
    def __init__(self, mesh):
        self.nd, self.nb, self.nh = (mesh.shape[axis] for axis in AXES)
        self.n = self.nd * self.nb * self.nh
        head_bits, blk_bits, dp_bits = (log2_of(size) for size in (self.nh, self.nb, self.nd))
        head = list(range(head_bits))
        blk = list(range(head_bits, head_bits + blk_bits))
        dp = list(range(head_bits + blk_bits, head_bits + blk_bits + dp_bits))
        self.orders = (dp + blk + head[1:] + head[:1], dp + head[1:] + blk + head[:1])
        self.phases = len(dp) + len(blk) + len(head)
        self.row = self.nb * self.nh
        self.groups = math.gcd(HEADS, self.row)
        self.split = self.row // self.groups

    def here(self):
        return (
            lax.axis_index("dp") * self.nb + lax.axis_index("blk")
        ) * self.nh + lax.axis_index("head")

    def coords(self, number):
        return (number // self.row, (number // self.nh) % self.nb, number % self.nh)

    def deltas(self, me, colour):
        steps = []
        for even, odd in zip(*self.orders):
            step = (1 - 2 * ((me // 2**even) % 2)) * 2**even
            if even != odd:
                other = (1 - 2 * ((me // 2**odd) % 2)) * 2**odd
                step = step + colour * (other - step)
            steps.append(step)
        return steps

    def plan(self):
        me = self.here()
        mine, other = self.deltas(me, me % 2), self.deltas(me, 1 - me % 2)

        def block(index):
            number = me
            use = other if index >> (self.phases - 1) & 1 else mine
            for bit in range(self.phases):
                if index >> bit & 1:
                    number = number + use[bit]
            return number

        return me, block, [self.coords(me + step) for step in mine]


def greet(devices):
    barrier = pltpu.get_barrier_semaphore()
    for device in devices:
        pl.semaphore_signal(barrier, 1, device_id=device, device_id_type=MESH_ID)
    pl.semaphore_wait(barrier, len(devices))


def remote(source, target, send, recv, device):
    return pltpu.make_async_remote_copy(
        src_ref=source,
        dst_ref=target,
        send_sem=send,
        recv_sem=recv,
        device_id=device,
        device_id_type=MESH_ID,
    )


def gather_steps(topo, ins, outs, send, recv, local):
    me, block, partner = topo.plan()
    phases = topo.phases
    sends = []

    def copy(k, index, phase):
        where = outs[k].at[block(index)]
        arrival = index + 2**phase
        return remote(
            ins[k] if index == 0 else where,
            where,
            send.at[k, arrival],
            recv.at[k, arrival],
            partner[phase],
        )

    def begin(k, index, phase):
        made = copy(k, index, phase)
        made.start()
        sends.append(made)

    for k in range(len(ins)):
        for phase in range(phases):
            begin(k, 0, phase)
    own = [pltpu.make_async_copy(ins[k], outs[k].at[me], local.at[k]) for k in range(len(ins))]
    for made in own:
        made.start()
    yield
    for index in range(1, 2**phases):
        top = index.bit_length() - 1
        where = block(index)
        for k in range(len(ins)):
            remote(
                outs[k].at[where],
                outs[k].at[where],
                send.at[k, index],
                recv.at[k, index],
                partner[top],
            ).wait_recv()
            for phase in range(top + 1, phases):
                begin(k, index, phase)
        yield
    for made in sends:
        made.wait_send()
    for made in own:
        made.wait()


def reduce_steps(topo, ins, outs, arrived, send, recv):
    me, block, partner = topo.plan()
    phases = topo.phases
    half = 2 ** (phases - 1)
    sends = []

    def copy(k, index, source):
        return remote(
            source,
            arrived[k].at[index],
            send.at[k, index],
            recv.at[k, index],
            partner[index.bit_length() - 1],
        )

    def begin(k, index, source):
        made = copy(k, index, source)
        made.start()
        sends.append(made)

    for index in range(2 * half - 1, half - 1, -1):
        for k in range(len(ins)):
            begin(k, index, ins[k].at[block(index)])
    yield
    for index in range(half - 1, -1, -1):
        top = index.bit_length() - 1
        where = block(index)
        for k in range(len(ins)):
            total = ins[k][where].astype(F32)
            for phase in range(phases - 1, top, -1):
                slot = arrived[k].at[2**phase + index]
                copy(k, 2**phase + index, slot).wait_recv()
                total = total + slot[...].astype(F32)
            if index == 0:
                outs[k][...] = total
            else:
                slot = arrived[k].at[half + index]
                slot[...] = total.astype(slot.dtype)
                begin(k, index, slot)
        yield
    for made in sends:
        made.wait_send()


def finish(steps):
    for _ in steps:
        pass


def gather_kernel(topo, count, *refs):
    ins, outs = refs[:count], refs[count : 2 * count]
    greet(topo.plan()[2])
    finish(gather_steps(topo, ins, outs, *refs[2 * count :]))


def comm_params(collective_id):
    return pltpu.CompilerParams(
        collective_id=collective_id, has_side_effects=True, vmem_limit_bytes=VMEM_LIMIT
    )


def dma(*shape):
    return pltpu.SemaphoreType.DMA(shape)


def in_vmem(count):
    return [pl.BlockSpec(memory_space=pltpu.VMEM)] * count


def in_any(count):
    return [pl.BlockSpec(memory_space=pl.ANY)] * count


def gathered_shapes(topo, arrays):
    return [jax.ShapeDtypeStruct((topo.n,) + a.shape, a.dtype) for a in arrays]


def gather_sems(topo, count):
    return [dma(count, topo.n), dma(count, topo.n), dma(count)]


def gather(topo, arrays, collective_id):
    count = len(arrays)
    return pl.pallas_call(
        partial(gather_kernel, topo, count),
        out_shape=gathered_shapes(topo, arrays),
        in_specs=in_vmem(count),
        out_specs=in_any(count),
        scratch_shapes=gather_sems(topo, count),
        compiler_params=comm_params(collective_id),
        name="gather",
    )(*arrays)


def reduce_kernel(topo, count, *refs):
    ins, outs, arrived = refs[:count], refs[count : 2 * count], refs[2 * count : 3 * count]
    greet(topo.plan()[2])
    finish(reduce_steps(topo, ins, outs, arrived, *refs[3 * count :]))


def owned_shapes(arrays):
    return [jax.ShapeDtypeStruct(a.shape[1:], F32) for a in arrays]


def arrival_scratch(arrays):
    return [pltpu.VMEM(a.shape, a.dtype) for a in arrays]


def reduce_sems(topo, count):
    return [dma(count, topo.n), dma(count, topo.n)]


def reduce_scatter(topo, arrays, collective_id):
    count = len(arrays)
    return pl.pallas_call(
        partial(reduce_kernel, topo, count),
        out_shape=owned_shapes(arrays),
        in_specs=in_vmem(count),
        out_specs=in_vmem(count),
        scratch_shapes=arrival_scratch(arrays) + reduce_sems(topo, count),
        compiler_params=comm_params(collective_id),
        name="reduce",
    )(*arrays)


def dot(left, right):
    return lax.dot_general(left, right, (((1,), (0,)), ((), ())), preferred_element_type=F32)


def repeat(count, step, state, tick):
    if count <= 8:
        for index in range(count):
            state = step(index, state)
            tick()
        return state
    return lax.fori_loop(0, count, step, state)


def span(index, size):
    if isinstance(index, int):
        return slice(index * size, (index + 1) * size)
    return pl.ds(pl.multiple_of(index * size, size), size)


def fit(total, most):
    return math.gcd(total, most)


def keys_with_mask(key_t, length):
    slots = key_t.shape[1]
    slot = lax.broadcasted_iota(jnp.int32, (slots, HEAD_DIM), 0)
    lane = lax.broadcasted_iota(jnp.int32, (slots, HEAD_DIM), 1)
    mask = jnp.where((lane == 0) & (slot >= length), NEG_LARGE, 0.0).astype(BF16)
    return jnp.concatenate([key_t.T, mask], axis=1)


def queries_with_one(query_t):
    row = lax.broadcasted_iota(jnp.int32, query_t.shape, 0)
    return jnp.concatenate([query_t, jnp.where(row == 0, 1.0, 0.0).astype(BF16)], axis=0)


def attend_head(head, length, qt, kt, vt, kn, scores, ot, low, lse, tick):
    slots, queries = kt.shape[1], qt.shape[1]
    width = scores.shape[1]
    step_keys = fit(slots, 256)
    rows = slice(head * HEAD_DIM, (head + 1) * HEAD_DIM)
    kn[...] = keys_with_mask(kt[rows, :], length)

    def one_width(index, _):
        columns = span(index, width)
        query = queries_with_one(qt[rows, columns])

        def find_peak(step, peak):
            keys = span(step, step_keys)
            part = dot(kn[keys, :], query)
            scores[keys, :] = part
            return jnp.maximum(peak, jnp.max(part, axis=0, keepdims=True))

        count = slots // step_keys
        peak = repeat(count, find_peak, jnp.full((1, width), NEG_LARGE, F32), tick)
        peak = peak * EXP2_SCALE

        def add_values(step, state):
            total, summed = state
            keys = span(step, step_keys)
            weights = jnp.exp2(scores[keys, :] * EXP2_SCALE - peak)
            total = total + jnp.sum(weights, axis=0, keepdims=True)
            return (total, summed + dot(vt[rows, keys], weights.astype(BF16)))

        start = (jnp.zeros((1, width), F32), jnp.zeros((HEAD_DIM, width), F32))
        total, summed = repeat(count, add_values, start, tick)
        output = summed / total
        ot[rows, columns] = output
        low[rows, columns] = output.astype(BF16)
        lse[head : head + 1, columns] = peak + jnp.log2(total)
        return 0

    if queries == width:
        one_width(0, 0)
    else:
        lax.fori_loop(0, queries // width, one_width, 0)


def attend_back_head(head, length, qt, kt, vt, gt, ot, lse, kn, vn, qn, gn, dq_sum, dq, dk, dv, tick):
    slots, queries = kt.shape[1], qt.shape[1]
    step_keys = fit(slots, 512)
    rows = slice(head * HEAD_DIM, (head + 1) * HEAD_DIM)
    kn[...] = keys_with_mask(kt[rows, :], length)
    vn[...] = vt[rows, :].T
    qn[...] = qt[rows, :].T
    gn[...] = gt[rows, :].T
    query = queries_with_one(qt[rows, :])
    grad = gt[rows, :]
    delta = jnp.sum(grad.astype(F32) * ot[rows, :], axis=0, keepdims=True)
    log_sum = lse[head : head + 1, :]
    dq_sum[...] = jnp.zeros_like(dq_sum)

    def one_step(step, _):
        keys = span(step, step_keys)
        weights = jnp.exp2(dot(kn[keys, :], query) * EXP2_SCALE - log_sum)
        grad_weights = dot(vn[keys, :], grad)
        grad_scores = (weights * (grad_weights - delta)).astype(BF16)
        dv[rows, keys] = dot(weights.astype(BF16), gn[...]).T.astype(BF16)
        dk[rows, keys] = (dot(grad_scores, qn[...]).T * SCORE_SCALE).astype(BF16)
        dq_sum[...] += dot(kt[rows, keys], grad_scores)
        return 0

    repeat(slots // step_keys, one_step, 0, tick)
    dq[rows, :] = (dq_sum[...] * SCORE_SCALE).astype(BF16)


class RowPlan:
    def __init__(self, topo):
        self.topo = topo
        self.groups, self.split = topo.groups, topo.split
        self.place = topo.here() % topo.row
        self.group, self.member = self.place // topo.split, self.place % topo.split

    def device(self, group, member):
        place = group * self.split + member
        topo = self.topo
        return (lax.axis_index("dp"), place // topo.nh, place % topo.nh)

    def across(self):
        return [(self.group + step) % self.groups for step in range(1, self.groups)]

    def beside(self):
        return [(self.member + step) % self.split for step in range(1, self.split)]

    def partners(self):
        return [self.device(group, self.member) for group in self.across()] + [
            self.device(self.group, member) for member in self.beside()
        ]


def columns_at(index, size):
    return pl.ds(pl.multiple_of(index * size, size), size)


def attend_kernel(topo, count, length_ref, qkv, *refs):
    shards, refs = refs[:count], refs[count:]
    attended, qt, kt, vt, ot, lse = refs[:6]
    outs, refs = refs[6 : 6 + count], refs[6 + count :]
    low, kn, scores, q_send, q_recv, kv_send, kv_recv, pass_send, back_send, back_recv, local = refs[:11]
    plan = RowPlan(topo)
    tokens = qkv.shape[3]
    greet(plan.partners() + topo.plan()[2])
    sends = []

    def begin(made):
        made.start()
        sends.append(made)

    own = plan.group * plan.split + plan.member
    full = (kt, vt)

    def slot_of(group, member):
        return columns_at(group * plan.split + member, tokens)

    for step, group in enumerate(plan.across()):
        device = plan.device(group, plan.member)
        for which in range(2):
            begin(
                remote(
                    qkv.at[1 + which, group],
                    full[which].at[:, slot_of(plan.group, plan.member)],
                    kv_send.at[which, step],
                    kv_recv.at[which, own],
                    device,
                )
            )
    for step, group in enumerate(plan.across()):
        begin(
            remote(
                qkv.at[0, group],
                qt.at[:, columns_at(plan.group, tokens)],
                q_send.at[step],
                q_recv.at[plan.group],
                plan.device(group, plan.member),
            )
        )
    mine = [
        pltpu.make_async_copy(
            qkv.at[0, plan.group], qt.at[:, columns_at(plan.group, tokens)], local.at[0]
        )
    ]
    for which in range(2):
        mine.append(
            pltpu.make_async_copy(
                qkv.at[1 + which, plan.group],
                full[which].at[:, slot_of(plan.group, plan.member)],
                local.at[1 + which],
            )
        )
    for made in mine:
        made.start()

    def hand_on(which, step, group, source):
        for index, member in enumerate(plan.beside()):
            begin(
                remote(
                    source,
                    full[which].at[:, slot_of(group, plan.member)],
                    pass_send.at[which, step, index],
                    kv_recv.at[which, group * plan.split + plan.member],
                    plan.device(plan.group, member),
                )
            )

    def wait_keys(which, group, member):
        where = full[which].at[:, slot_of(group, member)]
        remote(
            where,
            where,
            kv_send.at[which, 0],
            kv_recv.at[which, group * plan.split + member],
            plan.device(group, plan.member),
        ).wait_recv()

    for which in range(2):
        hand_on(which, 0, plan.group, qkv.at[1 + which, plan.group])
    weights = gather_steps(topo, shards, outs, *refs[11:])
    next(weights)

    def tick():
        next(weights, None)

    for step, group in enumerate(plan.across()):
        for which in range(2):
            wait_keys(which, group, plan.member)
            hand_on(
                which, step + 1, group, full[which].at[:, slot_of(group, plan.member)]
            )
        tick()
    for member in plan.beside():
        for group in [plan.group] + plan.across():
            for which in range(2):
                wait_keys(which, group, member)
    for step, group in enumerate(plan.across()):
        where = qt.at[:, columns_at(group, tokens)]
        remote(
            where, where, q_send.at[step], q_recv.at[group], plan.device(group, plan.member)
        ).wait_recv()
    for made in mine:
        made.wait()

    heads = qt.shape[0] // HEAD_DIM
    lse[...] = jnp.zeros_like(lse)
    returned = []
    for head in range(heads):
        attend_head(head, length_ref[0], qt, kt, vt, kn, scores, ot, low, lse, tick)
        rows = pl.ds(head * HEAD_DIM, HEAD_DIM)
        for step, group in enumerate(plan.across()):
            begin(
                remote(
                    low.at[rows, columns_at(group, tokens)],
                    attended.at[plan.group, rows],
                    back_send.at[head, step],
                    back_recv.at[head, plan.group],
                    plan.device(group, plan.member),
                )
            )
    made = pltpu.make_async_copy(
        low.at[:, columns_at(plan.group, tokens)], attended.at[plan.group], local.at[0]
    )
    made.start()
    finish(weights)
    made.wait()
    for head in range(heads):
        rows = pl.ds(head * HEAD_DIM, HEAD_DIM)
        for step, group in enumerate(plan.across()):
            where = attended.at[group, rows]
            remote(
                where,
                where,
                back_send.at[head, step],
                back_recv.at[head, group],
                plan.device(group, plan.member),
            ).wait_recv()
    for made in sends:
        made.wait_send()


def attend(topo, lengths, qkv, shards, slots, collective_id):
    count = len(shards)
    groups, split = topo.groups, topo.split
    width, tokens = qkv.shape[2:]
    heads = width // HEAD_DIM
    queries = groups * tokens
    score_width = fit(queries, max(128, 2**21 // slots))
    shapes = [
        jax.ShapeDtypeStruct((groups, width, tokens), BF16),
        jax.ShapeDtypeStruct((width, queries), BF16),
        jax.ShapeDtypeStruct((width, slots), BF16),
        jax.ShapeDtypeStruct((width, slots), BF16),
        jax.ShapeDtypeStruct((width, queries), F32),
        jax.ShapeDtypeStruct((8, queries), F32),
    ]
    results = pl.pallas_call(
        partial(attend_kernel, topo, count),
        out_shape=shapes + gathered_shapes(topo, shards),
        in_specs=[pl.BlockSpec(memory_space=pltpu.SMEM)] + in_vmem(1 + count),
        out_specs=in_vmem(len(shapes)) + in_any(count),
        scratch_shapes=[
            pltpu.VMEM((width, queries), BF16),
            pltpu.VMEM((slots, 2 * HEAD_DIM), BF16),
            pltpu.VMEM((slots, score_width), F32),
            dma(groups),
            dma(groups),
            dma(2, groups),
            dma(2, groups * split),
            dma(2, groups, split),
            dma(heads, groups),
            dma(heads, groups),
            dma(3),
        ]
        + gather_sems(topo, count),
        compiler_params=comm_params(collective_id),
        name="attend",
    )(lengths, qkv, *shards)
    return results[: len(shapes)], results[len(shapes) :]


def attend_back_kernel(topo, count, length_ref, grad, qt, kt, vt, ot, lse, *refs):
    terms, refs = refs[:count], refs[count:]
    back, owned, refs = refs[0], refs[1 : 1 + count], refs[1 + count :]
    gt, dq, dk, dv, partial_sums, kn, vn, qn, gn, dq_sum, refs = *refs[:10], refs[10:]
    g_send, g_recv, part_send, part_recv, back_send, back_recv, local = refs[:7]
    arrived, refs = refs[7 : 7 + count], refs[7 + count :]
    plan = RowPlan(topo)
    tokens = grad.shape[2]
    greet(plan.partners() + (topo.plan()[2] if count else []))
    sends = []

    def begin(made):
        made.start()
        sends.append(made)

    for step, group in enumerate(plan.across()):
        begin(
            remote(
                grad.at[group],
                gt.at[:, columns_at(plan.group, tokens)],
                g_send.at[step],
                g_recv.at[plan.group],
                plan.device(group, plan.member),
            )
        )
    mine = pltpu.make_async_copy(
        grad.at[plan.group], gt.at[:, columns_at(plan.group, tokens)], local.at[0]
    )
    mine.start()
    sums = reduce_steps(topo, terms, owned, arrived, *refs) if count else iter(())
    next(sums, None)

    def tick():
        next(sums, None)

    for step, group in enumerate(plan.across()):
        where = gt.at[:, columns_at(group, tokens)]
        remote(
            where, where, g_send.at[step], g_recv.at[group], plan.device(group, plan.member)
        ).wait_recv()
    mine.wait()
    heads = qt.shape[0] // HEAD_DIM
    pairs = (dk, dv)

    def slot_of(group, member):
        return columns_at(group * plan.split + member, tokens)

    for head in range(heads):
        attend_back_head(
            head, length_ref[0], qt, kt, vt, gt, ot, lse, kn, vn, qn, gn, dq_sum, dq, dk, dv, tick
        )
        rows = pl.ds(head * HEAD_DIM, HEAD_DIM)
        for index, member in enumerate(plan.beside()):
            for group in range(plan.groups):
                for which in range(2):
                    begin(
                        remote(
                            pairs[which].at[rows, slot_of(group, member)],
                            partial_sums.at[plan.split - 2 - index, which, group, rows],
                            part_send.at[head, which, group, index],
                            part_recv.at[head, which, group, plan.split - 2 - index],
                            plan.device(plan.group, member),
                        )
                    )
        for step, group in enumerate(plan.across()):
            begin(
                remote(
                    dq.at[rows, columns_at(group, tokens)],
                    back.at[0, plan.group, rows],
                    back_send.at[head, 0, step],
                    back_recv.at[head, 0, plan.group],
                    plan.device(group, plan.member),
                )
            )
    for head in range(heads):
        rows = pl.ds(head * HEAD_DIM, HEAD_DIM)
        for step, group in enumerate(plan.across() + [plan.group]):
            for which in range(2):
                where = pairs[which].at[rows, slot_of(group, plan.member)]
                total = where[...].astype(F32)
                for index, member in enumerate(plan.beside()):
                    slot = partial_sums.at[index, which, group, rows]
                    remote(
                        slot,
                        slot,
                        part_send.at[head, which, group, index],
                        part_recv.at[head, which, group, index],
                        plan.device(plan.group, member),
                    ).wait_recv()
                    total = total + slot[...].astype(F32)
                where[...] = total.astype(BF16)
                if step < plan.groups - 1:
                    begin(
                        remote(
                            where,
                            back.at[1 + which, plan.group, rows],
                            back_send.at[head, 1 + which, step],
                            back_recv.at[head, 1 + which, plan.group],
                            plan.device(group, plan.member),
                        )
                    )
            tick()
    back[0, plan.group] = dq[:, columns_at(plan.group, tokens)]
    for which in range(2):
        back[1 + which, plan.group] = pairs[which][:, slot_of(plan.group, plan.member)]
    finish(sums)
    for head in range(heads):
        rows = pl.ds(head * HEAD_DIM, HEAD_DIM)
        for which in range(3):
            for step, group in enumerate(plan.across()):
                where = back.at[which, group, rows]
                remote(
                    where,
                    where,
                    back_send.at[head, which, step],
                    back_recv.at[head, which, group],
                    plan.device(group, plan.member),
                ).wait_recv()
    for made in sends:
        made.wait_send()


def attend_back(topo, lengths, grad, saved, terms, collective_id):
    count = len(terms)
    groups, split = topo.groups, topo.split
    width, tokens = grad.shape[1:]
    heads = width // HEAD_DIM
    queries, slots = saved[0].shape[1], saved[1].shape[1]
    results = pl.pallas_call(
        partial(attend_back_kernel, topo, count),
        out_shape=[jax.ShapeDtypeStruct((3, groups, width, tokens), BF16)] + owned_shapes(terms),
        in_specs=[pl.BlockSpec(memory_space=pltpu.SMEM)] + in_vmem(1 + len(saved) + count),
        out_specs=in_vmem(1 + count),
        scratch_shapes=[
            pltpu.VMEM((width, queries), BF16),
            pltpu.VMEM((width, queries), BF16),
            pltpu.VMEM((width, slots), BF16),
            pltpu.VMEM((width, slots), BF16),
            pltpu.VMEM((max(split - 1, 1), 2, groups, width, tokens), BF16),
            pltpu.VMEM((slots, 2 * HEAD_DIM), BF16),
            pltpu.VMEM((slots, HEAD_DIM), BF16),
            pltpu.VMEM((queries, HEAD_DIM), BF16),
            pltpu.VMEM((queries, HEAD_DIM), BF16),
            pltpu.VMEM((HEAD_DIM, queries), F32),
            dma(groups),
            dma(groups),
            dma(heads, 2, groups, split),
            dma(heads, 2, groups, split),
            dma(heads, 3, groups),
            dma(heads, 3, groups),
            dma(1),
        ]
        + arrival_scratch(terms)
        + (reduce_sems(topo, count) if count else []),
        compiler_params=comm_params(collective_id),
        name="attend_back",
    )(lengths, grad, *saved, *terms)
    return results[0], results[1:]


def rotary_tables(positions):
    half_dim = HEAD_DIM // 2
    frequency = jnp.exp(
        jnp.arange(half_dim, dtype=F32) * (-2.0 * math.log(10000.0) / HEAD_DIM)
    )
    angles = frequency[:, None] * positions.astype(F32)[None, :]
    return (jnp.cos(angles), jnp.sin(angles))


def rotate(values, cosine, sine):
    first_half, second_half = jnp.split(values, 2, axis=1)
    return jnp.concatenate(
        [
            first_half * cosine - second_half * sine,
            second_half * cosine + first_half * sine,
        ],
        axis=1,
    )


def normalize(values):
    center = values - jnp.mean(values, axis=-1, keepdims=True)
    inverse = lax.rsqrt(jnp.mean(center * center, axis=-1, keepdims=True) + EPSILON)
    return (center * inverse, inverse)


def normalize_back(grad_unit, unit_values, inverse):
    mean_grad = jnp.mean(grad_unit, axis=-1, keepdims=True)
    mean_cross = jnp.mean(grad_unit * unit_values, axis=-1, keepdims=True)
    return (grad_unit - mean_grad - unit_values * mean_cross) * inverse


def product(equation, left, right):
    return jnp.einsum(equation, left, right, preferred_element_type=F32)


def joined(blocks):
    return blocks.reshape(-1, blocks.shape[-1])


def body(
    topo,
    tokens,
    cond,
    lengths,
    ada_weight,
    ada_bias,
    norm1_gain,
    qkv_weight,
    out_weight,
    norm2_gain,
    up_weight,
    up_bias,
    down_weight,
    down_bias,
    out_grad,
):
    devices = topo.n
    rows_all = topo.nd
    _, tok_count, width = tokens.shape
    slots = tok_count * topo.row
    cond_all = lax.all_gather(cond, "dp", axis=0, tiled=True)
    mod_columns = ada_weight.shape[1]
    mod_own = jnp.dot(cond_all, ada_weight, preferred_element_type=F32) + ada_bias.astype(F32)
    vectors = [norm1_gain, norm2_gain, up_bias, down_bias]
    small = jnp.concatenate([mod_own.reshape(-1)] + [v.astype(F32) for v in vectors])
    small = jnp.pad(small, (0, -small.shape[0] % 1024)).reshape(-1, 128)
    small_all, qkv_t = gather(topo, [small, qkv_weight.T], 0)
    qkv_t = joined(qkv_t)
    small_all = small_all.reshape(devices, -1)
    mod_all = small_all[:, : rows_all * mod_columns].reshape(devices, rows_all, mod_columns)
    modulation = lax.dynamic_index_in_dim(
        mod_all, lax.axis_index("dp"), 1, keepdims=False
    ).reshape(6, 1, width)
    shift_one, scale_one, gate_one, shift_two, scale_two, gate_two = modulation
    cut = rows_all * mod_columns
    full_vectors = []
    for v in vectors:
        full_vectors.append(small_all[:, cut : cut + v.shape[0]].reshape(-1))
        cut += v.shape[0]
    gain_one, gain_two, up_bias_full, down_bias_full = full_vectors
    seq_index = lax.axis_index("blk") * topo.nh + lax.axis_index("head")
    positions = seq_index * tok_count + jnp.arange(tok_count, dtype=jnp.int32)
    slot_live = (positions < lengths[0]).astype(F32)[:, None]
    cosine, sine = rotary_tables(positions)
    tokens_wide = tokens[0].astype(F32)
    unit_one, inverse_one = normalize(tokens_wide)
    normed_one = unit_one * gain_one
    hidden_one = (normed_one * (1.0 + scale_one) + shift_one).astype(BF16)
    projected = product("ed,td->et", qkv_t, hidden_one).reshape(
        3, HEADS, HEAD_DIM, tok_count
    )
    turned = jnp.stack(
        [rotate(projected[0], cosine, sine), rotate(projected[1], cosine, sine), projected[2]]
    ).astype(BF16)
    (attended, *saved), weights = attend(
        topo,
        lengths,
        turned.reshape(3, topo.groups, -1, tok_count),
        [out_weight.T, up_weight.T, down_weight.T, ada_weight.T],
        slots,
        1,
    )
    out_t, up_t, down_t, ada_t = (joined(w) for w in weights)
    attended = joined(attended)
    branch_one = product("dt,ed->te", attended, out_t)
    middle = tokens_wide + gate_one * branch_one
    unit_two, inverse_two = normalize(middle)
    normed_two = unit_two * gain_two
    hidden_two = (normed_two * (1.0 + scale_two) + shift_two).astype(BF16)
    inner = product("td,fd->tf", hidden_two, up_t) + up_bias_full
    activated, gelu_back = jax.vjp(partial(jax.nn.gelu, approximate=True), inner)
    activated = activated.astype(BF16)
    branch_two = product("tf,df->td", activated, down_t) + down_bias_full
    result = middle + gate_two * branch_two
    grad_out = out_grad[0].astype(F32) * slot_live
    grad_gate_two = jnp.sum(grad_out * branch_two, axis=0)
    grad_branch_two = (grad_out * gate_two).astype(BF16)
    grad_down = product("td,tf->df", grad_branch_two, activated)
    grad_down_bias = jnp.sum(grad_branch_two.astype(F32), axis=0)
    grad_activated = product("td,df->tf", grad_branch_two, down_t)
    grad_inner = gelu_back(grad_activated)[0].astype(BF16)
    grad_up = product("tf,td->fd", grad_inner, hidden_two)
    grad_up_bias = jnp.sum(grad_inner.astype(F32), axis=0)
    grad_hidden_two = product("tf,fd->td", grad_inner, up_t)
    grad_shift_two = jnp.sum(grad_hidden_two, axis=0)
    grad_scale_two = jnp.sum(grad_hidden_two * normed_two, axis=0)
    grad_normed_two = grad_hidden_two * (1.0 + scale_two)
    grad_gain_two = jnp.sum(grad_normed_two * unit_two, axis=0)
    grad_middle = grad_out + normalize_back(grad_normed_two * gain_two, unit_two, inverse_two)
    grad_gate_one = jnp.sum(grad_middle * branch_one, axis=0)
    grad_branch_one = (grad_middle * gate_one).astype(BF16)
    grad_out_proj = product("te,dt->ed", grad_branch_one, attended)
    grad_attended = product("ed,te->dt", out_t, grad_branch_one).astype(BF16)
    terms = [
        g.astype(BF16).reshape(devices, -1, g.shape[-1])
        for g in (grad_out_proj, grad_up, grad_down)
    ]
    fused = slots <= 4096
    grad_heads, owned = attend_back(
        topo,
        lengths,
        grad_attended.reshape(topo.groups, -1, tok_count),
        saved,
        terms if fused else [],
        2,
    )
    if not fused:
        owned = reduce_scatter(topo, terms, 3)
    out_own, up_own, down_own = owned
    grad_heads = grad_heads.reshape(3, HEADS, HEAD_DIM, tok_count)
    turned_back = [rotate(grad_heads[i].astype(F32), cosine, -sine) for i in range(2)]
    grad_projected = jnp.stack([turned_back[0], turned_back[1], grad_heads[2].astype(F32)])
    grad_projected = grad_projected.astype(BF16).reshape(-1, tok_count)
    grad_qkv = product("et,td->ed", grad_projected, hidden_one)
    grad_hidden_one = product("et,ed->td", grad_projected, qkv_t)
    grad_shift_one = jnp.sum(grad_hidden_one, axis=0)
    grad_scale_one = jnp.sum(grad_hidden_one * normed_one, axis=0)
    grad_normed_one = grad_hidden_one * (1.0 + scale_one)
    grad_gain_one = jnp.sum(grad_normed_one * unit_one, axis=0)
    grad_tokens = grad_middle + normalize_back(grad_normed_one * gain_one, unit_one, inverse_one)
    grad_modulation = jnp.concatenate(
        [
            grad_shift_one,
            grad_scale_one,
            grad_gate_one,
            grad_shift_two,
            grad_scale_two,
            grad_gate_two,
        ],
    )
    cond_part = jnp.dot(grad_modulation[None], ada_t.astype(F32), precision=HIGHEST)
    row_here = jnp.arange(rows_all, dtype=jnp.int32) == lax.axis_index("dp")
    plane = jnp.repeat(row_here, topo.row)
    mod_blocks = jnp.where(
        row_here[None, :, None], grad_modulation.reshape(devices, 1, mod_columns), 0.0
    )
    small_grads = jnp.concatenate(
        [mod_blocks.reshape(devices, -1)]
        + [
            v.reshape(devices, -1)
            for v in (grad_gain_one, grad_gain_two, grad_up_bias, grad_down_bias)
        ]
        + [jnp.where(plane[:, None], cond_part, 0.0)],
        axis=1,
    )
    small_grads = jnp.pad(small_grads, ((0, 0), (0, -small_grads.shape[1] % 1024)))
    small_own, qkv_own = reduce_scatter(
        topo,
        [
            small_grads.reshape(devices, -1, 128),
            grad_qkv.astype(BF16).reshape(devices, -1, grad_qkv.shape[-1]),
        ],
        4,
    )
    small_own = small_own.reshape(-1)
    cut = rows_all * mod_columns
    mod_grads = small_own[:cut].reshape(rows_all, mod_columns)
    vector_grads = []
    for v in vectors:
        vector_grads.append(small_own[cut : cut + v.shape[0]])
        cut += v.shape[0]
    grad_cond = small_own[cut : cut + cond.shape[1]].reshape(1, -1)
    grad_ada = jnp.dot(cond_all.astype(F32).T, mod_grads, precision=HIGHEST)
    return (
        result.astype(BF16)[None],
        grad_tokens[None],
        grad_cond,
        grad_ada,
        jnp.sum(mod_grads, axis=0),
        vector_grads[0],
        qkv_own.T,
        out_own.T,
        vector_grads[1],
        up_own.T,
        vector_grads[2],
        down_own.T,
        vector_grads[3],
    )


def solution(mesh):
    rows, owners = P("dp", ("blk", "head"), None), ("dp", "blk", "head")
    matrix, vector = P(None, owners), P(owners)
    params = [matrix, vector, vector, matrix, matrix, vector, matrix, vector, matrix, vector]
    return jax.shard_map(
        partial(body, Topo(mesh)),
        mesh=mesh,
        in_specs=(rows, P("dp", None), P("dp"), *params, rows),
        out_specs=(rows, rows, P("dp", None), *params),
        check_vma=False,
    )
```

```python
from functools import partial
import math

import jax
import jax.numpy as jnp
from jax import lax
from jax.experimental import pallas as pl
from jax.experimental.pallas import tpu as pltpu
from jax.sharding import PartitionSpec as P

HEADS = 12
HEAD_DIM = 64
EPSILON = 1e-05
NEG_LARGE = -1e30
HIGHEST = lax.Precision.HIGHEST
F32 = jnp.float32
BF16 = jnp.bfloat16
AXES = ("dp", "blk", "head")
MESH_ID = pl.DeviceIdType.MESH
SCORE_SCALE = HEAD_DIM ** (-0.5)
EXP2_SCALE = SCORE_SCALE * math.log2(math.e)
VMEM_LIMIT = 60 * 2**20


def log2_of(count):
    assert count & (count - 1) == 0
    return count.bit_length() - 1


class Topo:
    def __init__(self, mesh):
        self.nd, self.nb, self.nh = (mesh.shape[axis] for axis in AXES)
        self.n = self.nd * self.nb * self.nh
        head_bits, blk_bits, dp_bits = (log2_of(size) for size in (self.nh, self.nb, self.nd))
        head = list(range(head_bits))
        blk = list(range(head_bits, head_bits + blk_bits))
        dp = list(range(head_bits + blk_bits, head_bits + blk_bits + dp_bits))
        self.orders = (dp + blk + head[1:] + head[:1], dp + head[1:] + blk + head[:1])
        self.phases = len(dp) + len(blk) + len(head)
        self.row = self.nb * self.nh
        self.groups = math.gcd(HEADS, self.row)
        self.split = self.row // self.groups

    def here(self):
        return (
            lax.axis_index("dp") * self.nb + lax.axis_index("blk")
        ) * self.nh + lax.axis_index("head")

    def coords(self, number):
        return (number // self.row, (number // self.nh) % self.nb, number % self.nh)

    def deltas(self, me, colour):
        steps = []
        for even, odd in zip(*self.orders):
            step = (1 - 2 * ((me // 2**even) % 2)) * 2**even
            if even != odd:
                other = (1 - 2 * ((me // 2**odd) % 2)) * 2**odd
                step = step + colour * (other - step)
            steps.append(step)
        return steps

    def plan(self):
        me = self.here()
        mine, other = self.deltas(me, me % 2), self.deltas(me, 1 - me % 2)

        def block(index):
            number = me
            use = other if index >> (self.phases - 1) & 1 else mine
            for bit in range(self.phases):
                if index >> bit & 1:
                    number = number + use[bit]
            return number

        return me, block, [self.coords(me + step) for step in mine]


def greet(devices):
    barrier = pltpu.get_barrier_semaphore()
    for device in devices:
        pl.semaphore_signal(barrier, 1, device_id=device, device_id_type=MESH_ID)
    pl.semaphore_wait(barrier, len(devices))


def remote(source, target, send, recv, device):
    return pltpu.make_async_remote_copy(
        src_ref=source,
        dst_ref=target,
        send_sem=send,
        recv_sem=recv,
        device_id=device,
        device_id_type=MESH_ID,
    )


def gather_steps(topo, ins, outs, send, recv, local):
    me, block, partner = topo.plan()
    phases = topo.phases
    sends = []

    def copy(k, index, phase):
        where = outs[k].at[block(index)]
        arrival = index + 2**phase
        return remote(
            ins[k] if index == 0 else where,
            where,
            send.at[k, arrival],
            recv.at[k, arrival],
            partner[phase],
        )

    def begin(k, index, phase):
        made = copy(k, index, phase)
        made.start()
        sends.append(made)

    for k in range(len(ins)):
        for phase in range(phases):
            begin(k, 0, phase)
    own = [pltpu.make_async_copy(ins[k], outs[k].at[me], local.at[k]) for k in range(len(ins))]
    for made in own:
        made.start()
    yield
    for index in range(1, 2**phases):
        top = index.bit_length() - 1
        where = block(index)
        for k in range(len(ins)):
            remote(
                outs[k].at[where],
                outs[k].at[where],
                send.at[k, index],
                recv.at[k, index],
                partner[top],
            ).wait_recv()
            for phase in range(top + 1, phases):
                begin(k, index, phase)
        yield
    for made in sends:
        made.wait_send()
    for made in own:
        made.wait()


def reduce_steps(topo, ins, outs, arrived, send, recv):
    me, block, partner = topo.plan()
    phases = topo.phases
    half = 2 ** (phases - 1)
    sends = []

    def copy(k, index, source):
        return remote(
            source,
            arrived[k].at[index],
            send.at[k, index],
            recv.at[k, index],
            partner[index.bit_length() - 1],
        )

    def begin(k, index, source):
        made = copy(k, index, source)
        made.start()
        sends.append(made)

    for index in range(2 * half - 1, half - 1, -1):
        for k in range(len(ins)):
            begin(k, index, ins[k].at[block(index)])
    yield
    for index in range(half - 1, -1, -1):
        top = index.bit_length() - 1
        where = block(index)
        for k in range(len(ins)):
            total = ins[k][where].astype(F32)
            for phase in range(phases - 1, top, -1):
                slot = arrived[k].at[2**phase + index]
                copy(k, 2**phase + index, slot).wait_recv()
                total = total + slot[...].astype(F32)
            if index == 0:
                outs[k][...] = total
            else:
                slot = arrived[k].at[half + index]
                slot[...] = total.astype(slot.dtype)
                begin(k, index, slot)
        yield
    for made in sends:
        made.wait_send()


def finish(steps):
    for _ in steps:
        pass


def gather_kernel(topo, count, *refs):
    ins, outs = refs[:count], refs[count : 2 * count]
    greet(topo.plan()[2])
    finish(gather_steps(topo, ins, outs, *refs[2 * count :]))


def comm_params(collective_id):
    return pltpu.CompilerParams(
        collective_id=collective_id, has_side_effects=True, vmem_limit_bytes=VMEM_LIMIT
    )


def dma(*shape):
    return pltpu.SemaphoreType.DMA(shape)


def in_vmem(count):
    return [pl.BlockSpec(memory_space=pltpu.VMEM)] * count


def in_any(count):
    return [pl.BlockSpec(memory_space=pl.ANY)] * count


def gathered_shapes(topo, arrays):
    return [jax.ShapeDtypeStruct((topo.n,) + a.shape, a.dtype) for a in arrays]


def gather_sems(topo, count):
    return [dma(count, topo.n), dma(count, topo.n), dma(count)]


def gather(topo, arrays, collective_id):
    count = len(arrays)
    return pl.pallas_call(
        partial(gather_kernel, topo, count),
        out_shape=gathered_shapes(topo, arrays),
        in_specs=in_vmem(count),
        out_specs=in_any(count),
        scratch_shapes=gather_sems(topo, count),
        compiler_params=comm_params(collective_id),
        name="gather",
    )(*arrays)


def reduce_kernel(topo, count, *refs):
    ins, outs, arrived = refs[:count], refs[count : 2 * count], refs[2 * count : 3 * count]
    greet(topo.plan()[2])
    finish(reduce_steps(topo, ins, outs, arrived, *refs[3 * count :]))


def owned_shapes(arrays):
    return [jax.ShapeDtypeStruct(a.shape[1:], F32) for a in arrays]


def arrival_scratch(arrays):
    return [pltpu.VMEM(a.shape, a.dtype) for a in arrays]


def reduce_sems(topo, count):
    return [dma(count, topo.n), dma(count, topo.n)]


def reduce_scatter(topo, arrays, collective_id):
    count = len(arrays)
    return pl.pallas_call(
        partial(reduce_kernel, topo, count),
        out_shape=owned_shapes(arrays),
        in_specs=in_vmem(count),
        out_specs=in_vmem(count),
        scratch_shapes=arrival_scratch(arrays) + reduce_sems(topo, count),
        compiler_params=comm_params(collective_id),
        name="reduce",
    )(*arrays)


def dot(left, right):
    return lax.dot_general(left, right, (((1,), (0,)), ((), ())), preferred_element_type=F32)


def repeat(count, step, state, tick):
    if count <= 8:
        for index in range(count):
            state = step(index, state)
            tick()
        return state
    return lax.fori_loop(0, count, step, state)


def span(index, size):
    if isinstance(index, int):
        return slice(index * size, (index + 1) * size)
    return pl.ds(pl.multiple_of(index * size, size), size)


def fit(total, most):
    return math.gcd(total, most)


def keys_with_mask(key_t, length):
    slots = key_t.shape[1]
    slot = lax.broadcasted_iota(jnp.int32, (slots, HEAD_DIM), 0)
    lane = lax.broadcasted_iota(jnp.int32, (slots, HEAD_DIM), 1)
    mask = jnp.where((lane == 0) & (slot >= length), NEG_LARGE, 0.0).astype(BF16)
    return jnp.concatenate([key_t.T, mask], axis=1)


def queries_with_one(query_t):
    row = lax.broadcasted_iota(jnp.int32, query_t.shape, 0)
    return jnp.concatenate([query_t, jnp.where(row == 0, 1.0, 0.0).astype(BF16)], axis=0)


def attend_head(head, length, qt, kt, vt, kn, scores, ot, low, lse, tick):
    slots, queries = kt.shape[1], qt.shape[1]
    width = scores.shape[1]
    step_keys = fit(slots, 256)
    rows = slice(head * HEAD_DIM, (head + 1) * HEAD_DIM)
    kn[...] = keys_with_mask(kt[rows, :], length)

    def one_width(index, _):
        columns = span(index, width)
        query = queries_with_one(qt[rows, columns])

        def find_peak(step, peak):
            keys = span(step, step_keys)
            part = dot(kn[keys, :], query)
            scores[keys, :] = part
            return jnp.maximum(peak, jnp.max(part, axis=0, keepdims=True))

        count = slots // step_keys
        peak = repeat(count, find_peak, jnp.full((1, width), NEG_LARGE, F32), tick)
        peak = peak * EXP2_SCALE

        def add_values(step, state):
            total, summed = state
            keys = span(step, step_keys)
            weights = jnp.exp2(scores[keys, :] * EXP2_SCALE - peak)
            total = total + jnp.sum(weights, axis=0, keepdims=True)
            return (total, summed + dot(vt[rows, keys], weights.astype(BF16)))

        start = (jnp.zeros((1, width), F32), jnp.zeros((HEAD_DIM, width), F32))
        total, summed = repeat(count, add_values, start, tick)
        output = summed / total
        ot[rows, columns] = output
        low[rows, columns] = output.astype(BF16)
        lse[head : head + 1, columns] = peak + jnp.log2(total)
        return 0

    if queries == width:
        one_width(0, 0)
    else:
        lax.fori_loop(0, queries // width, one_width, 0)


def attend_back_head(head, length, qt, kt, vt, gt, ot, lse, kn, vn, qn, gn, dq_sum, dq, dk, dv, tick):
    slots, queries = kt.shape[1], qt.shape[1]
    step_keys = fit(slots, 512)
    rows = slice(head * HEAD_DIM, (head + 1) * HEAD_DIM)
    kn[...] = keys_with_mask(kt[rows, :], length)
    vn[...] = vt[rows, :].T
    qn[...] = qt[rows, :].T
    gn[...] = gt[rows, :].T
    query = queries_with_one(qt[rows, :])
    grad = gt[rows, :]
    delta = jnp.sum(grad.astype(F32) * ot[rows, :], axis=0, keepdims=True)
    log_sum = lse[head : head + 1, :]
    dq_sum[...] = jnp.zeros_like(dq_sum)

    def one_step(step, _):
        keys = span(step, step_keys)
        weights = jnp.exp2(dot(kn[keys, :], query) * EXP2_SCALE - log_sum)
        grad_weights = dot(vn[keys, :], grad)
        grad_scores = (weights * (grad_weights - delta)).astype(BF16)
        dv[rows, keys] = dot(weights.astype(BF16), gn[...]).T.astype(BF16)
        dk[rows, keys] = (dot(grad_scores, qn[...]).T * SCORE_SCALE).astype(BF16)
        dq_sum[...] += dot(kt[rows, keys], grad_scores)
        return 0

    repeat(slots // step_keys, one_step, 0, tick)
    dq[rows, :] = (dq_sum[...] * SCORE_SCALE).astype(BF16)


class RowPlan:
    def __init__(self, topo):
        self.topo = topo
        self.groups, self.split = topo.groups, topo.split
        self.place = topo.here() % topo.row
        self.group, self.member = self.place // topo.split, self.place % topo.split

    def device(self, group, member):
        place = group * self.split + member
        topo = self.topo
        return (lax.axis_index("dp"), place // topo.nh, place % topo.nh)

    def across(self):
        return [(self.group + step) % self.groups for step in range(1, self.groups)]

    def beside(self):
        return [(self.member + step) % self.split for step in range(1, self.split)]

    def partners(self):
        return [self.device(group, self.member) for group in self.across()] + [
            self.device(self.group, member) for member in self.beside()
        ]


def columns_at(index, size):
    return pl.ds(pl.multiple_of(index * size, size), size)


def attend_kernel(topo, count, length_ref, qkv, *refs):
    shards, refs = refs[:count], refs[count:]
    attended, qt, kt, vt, ot, lse = refs[:6]
    outs, refs = refs[6 : 6 + count], refs[6 + count :]
    low, kn, scores, q_send, q_recv, kv_send, kv_recv, pass_send, back_send, back_recv, local = refs[:11]
    plan = RowPlan(topo)
    tokens = qkv.shape[3]
    greet(plan.partners() + topo.plan()[2])
    sends = []

    def begin(made):
        made.start()
        sends.append(made)

    own = plan.group * plan.split + plan.member
    full = (kt, vt)

    def slot_of(group, member):
        return columns_at(group * plan.split + member, tokens)

    for step, group in enumerate(plan.across()):
        device = plan.device(group, plan.member)
        for which in range(2):
            begin(
                remote(
                    qkv.at[1 + which, group],
                    full[which].at[:, slot_of(plan.group, plan.member)],
                    kv_send.at[which, step],
                    kv_recv.at[which, own],
                    device,
                )
            )
    for step, group in enumerate(plan.across()):
        begin(
            remote(
                qkv.at[0, group],
                qt.at[:, columns_at(plan.group, tokens)],
                q_send.at[step],
                q_recv.at[plan.group],
                plan.device(group, plan.member),
            )
        )
    mine = [
        pltpu.make_async_copy(
            qkv.at[0, plan.group], qt.at[:, columns_at(plan.group, tokens)], local.at[0]
        )
    ]
    for which in range(2):
        mine.append(
            pltpu.make_async_copy(
                qkv.at[1 + which, plan.group],
                full[which].at[:, slot_of(plan.group, plan.member)],
                local.at[1 + which],
            )
        )
    for made in mine:
        made.start()

    def hand_on(which, step, group, source):
        for index, member in enumerate(plan.beside()):
            begin(
                remote(
                    source,
                    full[which].at[:, slot_of(group, plan.member)],
                    pass_send.at[which, step, index],
                    kv_recv.at[which, group * plan.split + plan.member],
                    plan.device(plan.group, member),
                )
            )

    def wait_keys(which, group, member):
        where = full[which].at[:, slot_of(group, member)]
        remote(
            where,
            where,
            kv_send.at[which, 0],
            kv_recv.at[which, group * plan.split + member],
            plan.device(group, plan.member),
        ).wait_recv()

    for which in range(2):
        hand_on(which, 0, plan.group, qkv.at[1 + which, plan.group])
    weights = gather_steps(topo, shards, outs, *refs[11:])
    next(weights)

    def tick():
        next(weights, None)

    for step, group in enumerate(plan.across()):
        for which in range(2):
            wait_keys(which, group, plan.member)
            hand_on(
                which, step + 1, group, full[which].at[:, slot_of(group, plan.member)]
            )
        tick()
    for member in plan.beside():
        for group in [plan.group] + plan.across():
            for which in range(2):
                wait_keys(which, group, member)
    for step, group in enumerate(plan.across()):
        where = qt.at[:, columns_at(group, tokens)]
        remote(
            where, where, q_send.at[step], q_recv.at[group], plan.device(group, plan.member)
        ).wait_recv()
    for made in mine:
        made.wait()

    heads = qt.shape[0] // HEAD_DIM
    lse[...] = jnp.zeros_like(lse)
    returned = []
    for head in range(heads):
        attend_head(head, length_ref[0], qt, kt, vt, kn, scores, ot, low, lse, tick)
        rows = pl.ds(head * HEAD_DIM, HEAD_DIM)
        for step, group in enumerate(plan.across()):
            begin(
                remote(
                    low.at[rows, columns_at(group, tokens)],
                    attended.at[plan.group, rows],
                    back_send.at[head, step],
                    back_recv.at[head, plan.group],
                    plan.device(group, plan.member),
                )
            )
    made = pltpu.make_async_copy(
        low.at[:, columns_at(plan.group, tokens)], attended.at[plan.group], local.at[0]
    )
    made.start()
    finish(weights)
    made.wait()
    for head in range(heads):
        rows = pl.ds(head * HEAD_DIM, HEAD_DIM)
        for step, group in enumerate(plan.across()):
            where = attended.at[group, rows]
            remote(
                where,
                where,
                back_send.at[head, step],
                back_recv.at[head, group],
                plan.device(group, plan.member),
            ).wait_recv()
    for made in sends:
        made.wait_send()


def attend(topo, lengths, qkv, shards, slots, collective_id):
    count = len(shards)
    groups, split = topo.groups, topo.split
    width, tokens = qkv.shape[2:]
    heads = width // HEAD_DIM
    queries = groups * tokens
    score_width = fit(queries, max(128, 2**21 // slots))
    shapes = [
        jax.ShapeDtypeStruct((groups, width, tokens), BF16),
        jax.ShapeDtypeStruct((width, queries), BF16),
        jax.ShapeDtypeStruct((width, slots), BF16),
        jax.ShapeDtypeStruct((width, slots), BF16),
        jax.ShapeDtypeStruct((width, queries), F32),
        jax.ShapeDtypeStruct((8, queries), F32),
    ]
    results = pl.pallas_call(
        partial(attend_kernel, topo, count),
        out_shape=shapes + gathered_shapes(topo, shards),
        in_specs=[pl.BlockSpec(memory_space=pltpu.SMEM)] + in_vmem(1 + count),
        out_specs=in_vmem(len(shapes)) + in_any(count),
        scratch_shapes=[
            pltpu.VMEM((width, queries), BF16),
            pltpu.VMEM((slots, 2 * HEAD_DIM), BF16),
            pltpu.VMEM((slots, score_width), F32),
            dma(groups),
            dma(groups),
            dma(2, groups),
            dma(2, groups * split),
            dma(2, groups, split),
            dma(heads, groups),
            dma(heads, groups),
            dma(3),
        ]
        + gather_sems(topo, count),
        compiler_params=comm_params(collective_id),
        name="attend",
    )(lengths, qkv, *shards)
    return results[: len(shapes)], results[len(shapes) :]


def attend_back_kernel(topo, count, length_ref, grad, qt, kt, vt, ot, lse, *refs):
    terms, refs = refs[:count], refs[count:]
    back, owned, refs = refs[0], refs[1 : 1 + count], refs[1 + count :]
    gt, dq, dk, dv, partial_sums, kn, vn, qn, gn, dq_sum, refs = *refs[:10], refs[10:]
    g_send, g_recv, part_send, part_recv, back_send, back_recv, local = refs[:7]
    arrived, refs = refs[7 : 7 + count], refs[7 + count :]
    plan = RowPlan(topo)
    tokens = grad.shape[2]
    greet(plan.partners() + (topo.plan()[2] if count else []))
    sends = []

    def begin(made):
        made.start()
        sends.append(made)

    for step, group in enumerate(plan.across()):
        begin(
            remote(
                grad.at[group],
                gt.at[:, columns_at(plan.group, tokens)],
                g_send.at[step],
                g_recv.at[plan.group],
                plan.device(group, plan.member),
            )
        )
    mine = pltpu.make_async_copy(
        grad.at[plan.group], gt.at[:, columns_at(plan.group, tokens)], local.at[0]
    )
    mine.start()
    sums = reduce_steps(topo, terms, owned, arrived, *refs) if count else iter(())
    next(sums, None)

    def tick():
        next(sums, None)

    for step, group in enumerate(plan.across()):
        where = gt.at[:, columns_at(group, tokens)]
        remote(
            where, where, g_send.at[step], g_recv.at[group], plan.device(group, plan.member)
        ).wait_recv()
    mine.wait()
    heads = qt.shape[0] // HEAD_DIM
    pairs = (dk, dv)

    def slot_of(group, member):
        return columns_at(group * plan.split + member, tokens)

    for head in range(heads):
        attend_back_head(
            head, length_ref[0], qt, kt, vt, gt, ot, lse, kn, vn, qn, gn, dq_sum, dq, dk, dv, tick
        )
        rows = pl.ds(head * HEAD_DIM, HEAD_DIM)
        for index, member in enumerate(plan.beside()):
            for group in range(plan.groups):
                for which in range(2):
                    begin(
                        remote(
                            pairs[which].at[rows, slot_of(group, member)],
                            partial_sums.at[plan.split - 2 - index, which, group, rows],
                            part_send.at[head, which, group, index],
                            part_recv.at[head, which, group, plan.split - 2 - index],
                            plan.device(plan.group, member),
                        )
                    )
        for step, group in enumerate(plan.across()):
            begin(
                remote(
                    dq.at[rows, columns_at(group, tokens)],
                    back.at[0, plan.group, rows],
                    back_send.at[head, 0, step],
                    back_recv.at[head, 0, plan.group],
                    plan.device(group, plan.member),
                )
            )
    for head in range(heads):
        rows = pl.ds(head * HEAD_DIM, HEAD_DIM)
        for step, group in enumerate(plan.across() + [plan.group]):
            for which in range(2):
                where = pairs[which].at[rows, slot_of(group, plan.member)]
                total = where[...].astype(F32)
                for index, member in enumerate(plan.beside()):
                    slot = partial_sums.at[index, which, group, rows]
                    remote(
                        slot,
                        slot,
                        part_send.at[head, which, group, index],
                        part_recv.at[head, which, group, index],
                        plan.device(plan.group, member),
                    ).wait_recv()
                    total = total + slot[...].astype(F32)
                where[...] = total.astype(BF16)
                if step < plan.groups - 1:
                    begin(
                        remote(
                            where,
                            back.at[1 + which, plan.group, rows],
                            back_send.at[head, 1 + which, step],
                            back_recv.at[head, 1 + which, plan.group],
                            plan.device(group, plan.member),
                        )
                    )
            tick()
    back[0, plan.group] = dq[:, columns_at(plan.group, tokens)]
    for which in range(2):
        back[1 + which, plan.group] = pairs[which][:, slot_of(plan.group, plan.member)]
    finish(sums)
    for head in range(heads):
        rows = pl.ds(head * HEAD_DIM, HEAD_DIM)
        for which in range(3):
            for step, group in enumerate(plan.across()):
                where = back.at[which, group, rows]
                remote(
                    where,
                    where,
                    back_send.at[head, which, step],
                    back_recv.at[head, which, group],
                    plan.device(group, plan.member),
                ).wait_recv()
    for made in sends:
        made.wait_send()


def attend_back(topo, lengths, grad, saved, terms, collective_id):
    count = len(terms)
    groups, split = topo.groups, topo.split
    width, tokens = grad.shape[1:]
    heads = width // HEAD_DIM
    queries, slots = saved[0].shape[1], saved[1].shape[1]
    results = pl.pallas_call(
        partial(attend_back_kernel, topo, count),
        out_shape=[jax.ShapeDtypeStruct((3, groups, width, tokens), BF16)] + owned_shapes(terms),
        in_specs=[pl.BlockSpec(memory_space=pltpu.SMEM)] + in_vmem(1 + len(saved) + count),
        out_specs=in_vmem(1 + count),
        scratch_shapes=[
            pltpu.VMEM((width, queries), BF16),
            pltpu.VMEM((width, queries), BF16),
            pltpu.VMEM((width, slots), BF16),
            pltpu.VMEM((width, slots), BF16),
            pltpu.VMEM((max(split - 1, 1), 2, groups, width, tokens), BF16),
            pltpu.VMEM((slots, 2 * HEAD_DIM), BF16),
            pltpu.VMEM((slots, HEAD_DIM), BF16),
            pltpu.VMEM((queries, HEAD_DIM), BF16),
            pltpu.VMEM((queries, HEAD_DIM), BF16),
            pltpu.VMEM((HEAD_DIM, queries), F32),
            dma(groups),
            dma(groups),
            dma(heads, 2, groups, split),
            dma(heads, 2, groups, split),
            dma(heads, 3, groups),
            dma(heads, 3, groups),
            dma(1),
        ]
        + arrival_scratch(terms)
        + (reduce_sems(topo, count) if count else []),
        compiler_params=comm_params(collective_id),
        name="attend_back",
    )(lengths, grad, *saved, *terms)
    return results[0], results[1:]


def rotary_tables(positions):
    half_dim = HEAD_DIM // 2
    frequency = jnp.exp(
        jnp.arange(half_dim, dtype=F32) * (-2.0 * math.log(10000.0) / HEAD_DIM)
    )
    angles = frequency[:, None] * positions.astype(F32)[None, :]
    return (jnp.cos(angles), jnp.sin(angles))


def rotate(values, cosine, sine):
    first_half, second_half = jnp.split(values, 2, axis=1)
    return jnp.concatenate(
        [
            first_half * cosine - second_half * sine,
            second_half * cosine + first_half * sine,
        ],
        axis=1,
    )


def normalize(values):
    center = values - jnp.mean(values, axis=-1, keepdims=True)
    inverse = lax.rsqrt(jnp.mean(center * center, axis=-1, keepdims=True) + EPSILON)
    return (center * inverse, inverse)


def normalize_back(grad_unit, unit_values, inverse):
    mean_grad = jnp.mean(grad_unit, axis=-1, keepdims=True)
    mean_cross = jnp.mean(grad_unit * unit_values, axis=-1, keepdims=True)
    return (grad_unit - mean_grad - unit_values * mean_cross) * inverse


def product(equation, left, right):
    return jnp.einsum(equation, left, right, preferred_element_type=F32)


def joined(blocks):
    return blocks.reshape(-1, blocks.shape[-1])


def body(
    topo,
    tokens,
    cond,
    lengths,
    ada_weight,
    ada_bias,
    norm1_gain,
    qkv_weight,
    out_weight,
    norm2_gain,
    up_weight,
    up_bias,
    down_weight,
    down_bias,
    out_grad,
):
    devices = topo.n
    rows_all = topo.nd
    _, tok_count, width = tokens.shape
    slots = tok_count * topo.row
    vectors = [norm1_gain, norm2_gain, up_bias, down_bias]
    mod_columns = ada_weight.shape[1]
    small = jnp.concatenate([v.astype(F32) for v in (cond[0], ada_bias, *vectors)])
    small = jnp.pad(small, (0, -small.shape[0] % 1024)).reshape(-1, 128)
    small_all, ada_t, qkv_t = gather(topo, [small, ada_weight.T, qkv_weight.T], 0)
    ada_t, qkv_t = joined(ada_t), joined(qkv_t)
    small_all = small_all.reshape(devices, -1)
    cond_all = small_all[:: topo.row, : cond.shape[1]]
    cut = cond.shape[1]
    full_vectors = []
    for v in (ada_bias, *vectors):
        full_vectors.append(small_all[:, cut : cut + v.shape[0]].reshape(-1))
        cut += v.shape[0]
    ada_bias_full, gain_one, gain_two, up_bias_full, down_bias_full = full_vectors
    modulation = (product("rc,ec->re", cond, ada_t) + ada_bias_full).reshape(6, 1, width)
    shift_one, scale_one, gate_one, shift_two, scale_two, gate_two = modulation
    seq_index = lax.axis_index("blk") * topo.nh + lax.axis_index("head")
    positions = seq_index * tok_count + jnp.arange(tok_count, dtype=jnp.int32)
    slot_live = (positions < lengths[0]).astype(F32)[:, None]
    cosine, sine = rotary_tables(positions)
    tokens_wide = tokens[0].astype(F32)
    unit_one, inverse_one = normalize(tokens_wide)
    normed_one = unit_one * gain_one
    hidden_one = (normed_one * (1.0 + scale_one) + shift_one).astype(BF16)
    projected = product("ed,td->et", qkv_t, hidden_one).reshape(
        3, HEADS, HEAD_DIM, tok_count
    )
    turned = jnp.stack(
        [rotate(projected[0], cosine, sine), rotate(projected[1], cosine, sine), projected[2]]
    ).astype(BF16)
    (attended, *saved), weights = attend(
        topo,
        lengths,
        turned.reshape(3, topo.groups, -1, tok_count),
        [out_weight.T, up_weight.T, down_weight.T],
        slots,
        1,
    )
    out_t, up_t, down_t = (joined(w) for w in weights)
    attended = joined(attended)
    branch_one = product("dt,ed->te", attended, out_t)
    middle = tokens_wide + gate_one * branch_one
    unit_two, inverse_two = normalize(middle)
    normed_two = unit_two * gain_two
    hidden_two = (normed_two * (1.0 + scale_two) + shift_two).astype(BF16)
    inner = product("td,fd->tf", hidden_two, up_t) + up_bias_full
    activated, gelu_back = jax.vjp(partial(jax.nn.gelu, approximate=True), inner)
    activated = activated.astype(BF16)
    branch_two = product("tf,df->td", activated, down_t) + down_bias_full
    result = middle + gate_two * branch_two
    grad_out = out_grad[0].astype(F32) * slot_live
    grad_gate_two = jnp.sum(grad_out * branch_two, axis=0)
    grad_branch_two = (grad_out * gate_two).astype(BF16)
    grad_down = product("td,tf->df", grad_branch_two, activated)
    grad_down_bias = jnp.sum(grad_branch_two.astype(F32), axis=0)
    grad_activated = product("td,df->tf", grad_branch_two, down_t)
    grad_inner = gelu_back(grad_activated)[0].astype(BF16)
    grad_up = product("tf,td->fd", grad_inner, hidden_two)
    grad_up_bias = jnp.sum(grad_inner.astype(F32), axis=0)
    grad_hidden_two = product("tf,fd->td", grad_inner, up_t)
    grad_shift_two = jnp.sum(grad_hidden_two, axis=0)
    grad_scale_two = jnp.sum(grad_hidden_two * normed_two, axis=0)
    grad_normed_two = grad_hidden_two * (1.0 + scale_two)
    grad_gain_two = jnp.sum(grad_normed_two * unit_two, axis=0)
    grad_middle = grad_out + normalize_back(grad_normed_two * gain_two, unit_two, inverse_two)
    grad_gate_one = jnp.sum(grad_middle * branch_one, axis=0)
    grad_branch_one = (grad_middle * gate_one).astype(BF16)
    grad_out_proj = product("te,dt->ed", grad_branch_one, attended)
    grad_attended = product("ed,te->dt", out_t, grad_branch_one).astype(BF16)
    terms = [
        g.astype(BF16).reshape(devices, -1, g.shape[-1])
        for g in (grad_out_proj, grad_up, grad_down)
    ]
    fused = slots <= 4096
    grad_heads, owned = attend_back(
        topo,
        lengths,
        grad_attended.reshape(topo.groups, -1, tok_count),
        saved,
        terms if fused else [],
        2,
    )
    if not fused:
        owned = reduce_scatter(topo, terms, 3)
    out_own, up_own, down_own = owned
    grad_heads = grad_heads.reshape(3, HEADS, HEAD_DIM, tok_count)
    turned_back = [rotate(grad_heads[i].astype(F32), cosine, -sine) for i in range(2)]
    grad_projected = jnp.stack([turned_back[0], turned_back[1], grad_heads[2].astype(F32)])
    grad_projected = grad_projected.astype(BF16).reshape(-1, tok_count)
    grad_qkv = product("et,td->ed", grad_projected, hidden_one)
    grad_hidden_one = product("et,ed->td", grad_projected, qkv_t)
    grad_shift_one = jnp.sum(grad_hidden_one, axis=0)
    grad_scale_one = jnp.sum(grad_hidden_one * normed_one, axis=0)
    grad_normed_one = grad_hidden_one * (1.0 + scale_one)
    grad_gain_one = jnp.sum(grad_normed_one * unit_one, axis=0)
    grad_tokens = grad_middle + normalize_back(grad_normed_one * gain_one, unit_one, inverse_one)
    grad_modulation = jnp.concatenate(
        [
            grad_shift_one,
            grad_scale_one,
            grad_gate_one,
            grad_shift_two,
            grad_scale_two,
            grad_gate_two,
        ],
    )
    cond_part = jnp.dot(grad_modulation[None], ada_t.astype(F32), precision=HIGHEST)
    row_here = jnp.arange(rows_all, dtype=jnp.int32) == lax.axis_index("dp")
    plane = jnp.repeat(row_here, topo.row)
    mod_blocks = jnp.where(
        row_here[None, :, None], grad_modulation.reshape(devices, 1, mod_columns), 0.0
    )
    small_grads = jnp.concatenate(
        [mod_blocks.reshape(devices, -1)]
        + [
            v.reshape(devices, -1)
            for v in (grad_gain_one, grad_gain_two, grad_up_bias, grad_down_bias)
        ]
        + [jnp.where(plane[:, None], cond_part, 0.0)],
        axis=1,
    )
    small_grads = jnp.pad(small_grads, ((0, 0), (0, -small_grads.shape[1] % 1024)))
    small_own, qkv_own = reduce_scatter(
        topo,
        [
            small_grads.reshape(devices, -1, 128),
            grad_qkv.astype(BF16).reshape(devices, -1, grad_qkv.shape[-1]),
        ],
        4,
    )
    small_own = small_own.reshape(-1)
    cut = rows_all * mod_columns
    mod_grads = small_own[:cut].reshape(rows_all, mod_columns)
    vector_grads = []
    for v in vectors:
        vector_grads.append(small_own[cut : cut + v.shape[0]])
        cut += v.shape[0]
    grad_cond = small_own[cut : cut + cond.shape[1]].reshape(1, -1)
    grad_ada = jnp.dot(cond_all.T, mod_grads, precision=HIGHEST)
    return (
        result.astype(BF16)[None],
        grad_tokens[None],
        grad_cond,
        grad_ada,
        jnp.sum(mod_grads, axis=0),
        vector_grads[0],
        qkv_own.T,
        out_own.T,
        vector_grads[1],
        up_own.T,
        vector_grads[2],
        down_own.T,
        vector_grads[3],
    )


def solution(mesh):
    rows, owners = P("dp", ("blk", "head"), None), ("dp", "blk", "head")
    matrix, vector = P(None, owners), P(owners)
    params = [matrix, vector, vector, matrix, matrix, vector, matrix, vector, matrix, vector]
    return jax.shard_map(
        partial(body, Topo(mesh)),
        mesh=mesh,
        in_specs=(rows, P("dp", None), P("dp"), *params, rows),
        out_specs=(rows, rows, P("dp", None), *params),
        check_vma=False,
    )
```
